32 devices in a mesh: dp: 8 (over z, x), seq: 4 (over y, core).
Axes of the slice: x: 2, y: 2, z: 4, core: 2. Of those that a mesh axis runs over, the one named last changes fastest.
Arguments:
- queries: bfloat16 [8, 512, 1024], P('dp', 'seq'), may hold values from -6 to 6
- key_vecs: bfloat16 [8, 512, 1024], P('dp', 'seq'), may hold values from -6 to 6
- value_vecs: bfloat16 [8, 512, 1024], P('dp', 'seq'), may hold values from -6 to 6
- residual_in: bfloat16 [8, 512, 1024], P('dp', 'seq'), may hold values from -8 to 8
- point_weight: bfloat16 [1024, 2048], P('seq'), may hold values from -0.5 to 0.5
- context_grad: bfloat16 [8, 512, 1024], P('dp', 'seq'), may hold values from -6 to 6
- depth_kernel: float32 [31, 1024], replicated, may hold values from -1 to 1
- norm_gain: float32 [1024], replicated, may hold values from 0.5 to 1.5
- norm_bias: float32 [1024], replicated, may hold values from -3 to 3
- conv_grad: bfloat16 [8, 512, 1024], P('dp', 'seq'), may hold values from -1.5 to 1.5
Outputs:
- context: bfloat16 [8, 512, 1024], P('dp', 'seq')
- conv_output: bfloat16 [8, 512, 1024], P('dp', 'seq')
- query_grad: bfloat16 [8, 512, 1024], P('dp', 'seq')
- key_grad: bfloat16 [8, 512, 1024], P('dp', 'seq')
- value_grad: bfloat16 [8, 512, 1024], P('dp', 'seq')
- input_grad: bfloat16 [8, 512, 2048], P('dp', 'seq')
- residual_grad: bfloat16 [8, 512, 1024], P('dp', 'seq')
- kernel_grad: float32 [31, 1024], replicated
- gain_grad: float32 [1024], replicated
- bias_grad: float32 [1024], replicated
The draws below stay inside these ranges and needn't reach their ends.
All inputs are finite; a program needn't handle non-finite values.
Results may differ from the reference program's by a relative error of at most 0.0049.
The reference program's roundings to bfloat16 on the way count: a program that leaves them out, or rounds other values in their place, can miss the bound.
Values may be sent and summed in bfloat16 or wider, within the bound.
A program may use at most 64 MiB of HBM per device.

```python
import math
import jax
import jax.numpy as jnp
from jax import lax

D = 1024
HEADS = 16
KERNEL = 31
HD = 64
FRAMES = 512
RECS = 8


def drawn_pair(key):
    query_key = jax.random.fold_in(key, 101)
    keys_key = jax.random.fold_in(key, 102)
    full_shape = (RECS, FRAMES, D)
    query_base = jnp.clip(jax.random.normal(query_key, full_shape, jnp.float32), -4.0, 4.0)
    key_base = jnp.clip(jax.random.normal(keys_key, full_shape, jnp.float32), -4.0, 4.0)
    return (query_base, key_base)


def draw_queries(key, part):
    return drawn_pair(key)[0].astype(jnp.bfloat16)


def draw_key_vecs(key, part):
    return drawn_pair(key)[1].astype(jnp.bfloat16)


def draw_residual_in(key, part):
    full_shape = (RECS, FRAMES, D)
    column_scale = jnp.exp(jax.random.uniform(jax.random.fold_in(key, 201), (1, 1, D), jnp.float32, 0.0, math.log(10.0))) * 0.5
    row_scale = jnp.exp(jax.random.uniform(jax.random.fold_in(key, 202), (RECS, FRAMES, 1), jnp.float32, 0.0, math.log(10.0))) * 0.5
    base_values = jax.random.normal(jax.random.fold_in(key, 203), full_shape, jnp.float32)
    return jnp.clip(base_values * column_scale * row_scale, -8.0, 8.0).astype(jnp.bfloat16)


def draw_point_weight(key, part):
    full_shape = (D, 2 * D)
    column_scale = jnp.exp(jax.random.uniform(jax.random.fold_in(key, 301), (1, 2 * D), jnp.float32, 0.0, math.log(10.0))) * 0.1
    base_values = jnp.clip(jax.random.normal(jax.random.fold_in(key, 302), full_shape, jnp.float32), -4.0, 4.0)
    return jnp.clip(base_values * column_scale * D ** (-0.5), -0.5, 0.5).astype(jnp.bfloat16)


def level_of(own_key, extent, shards, low, high):
    factor_of = 1.0
    for position, parts in shards:
        steps = jax.random.uniform(jax.random.fold_in(jax.random.fold_in(own_key, 6), position), (parts,), jnp.float32, low / len(shards), high / len(shards))
        factor_of = factor_of * jnp.repeat(jnp.exp(steps), extent[position] // parts).reshape((-1,) + (1,) * (len(extent) - 1 - position))
    return factor_of


def centred(rng, shape, width, limit, cuts=(), held_as=jnp.bfloat16):
    level = level_of(rng, shape, cuts, -0.22, 0.18) if cuts else 1.0
    drawn = jax.random.normal(rng, shape, jnp.float32) * width * level
    return jnp.minimum(jnp.maximum(drawn, -limit), limit).astype(held_as)


def setup_inputs(seed: int = 0) -> dict:
    splits = jax.random.split(jax.random.key(seed), 11)
    queries = draw_queries(jax.random.fold_in(splits[10], 71), 0)
    key_vecs = draw_key_vecs(jax.random.fold_in(splits[10], 71), 0)
    value_vecs = centred(splits[2], (RECS, FRAMES, D), 1.0, 6.0, ((0, 8), (1, 4)))
    residual_in = draw_residual_in(jax.random.fold_in(splits[10], 71), 0)
    point_weight = draw_point_weight(jax.random.fold_in(splits[10], 71), 0)
    context_grad = centred(splits[5], (RECS, FRAMES, D), 1.0, 6.0, ((0, 8), (1, 4)))
    depth_kernel = centred(splits[6], (KERNEL, D), KERNEL ** -0.5, 1.0, (), jnp.float32)
    norm_gain = jnp.clip(1.0 + 0.1 * jax.random.normal(splits[7], (D,), jnp.float32), 0.5, 1.5)
    norm_bias = centred(splits[8], (D,), 0.5, 3.0, (), jnp.float32)
    conv_grad = centred(splits[9], (RECS, FRAMES, D), 0.25, 1.5, ((0, 8), (1, 4)))
    return dict(queries=queries, key_vecs=key_vecs, value_vecs=value_vecs, residual_in=residual_in, point_weight=point_weight, context_grad=context_grad, depth_kernel=depth_kernel, norm_gain=norm_gain, norm_bias=norm_bias, conv_grad=conv_grad)


def to_heads(array):
    return array.reshape(RECS, FRAMES, HEADS, HD).transpose(0, 2, 1, 3).reshape(RECS * HEADS, FRAMES, HD)

def from_heads(array):
    return array.reshape(RECS, HEADS, FRAMES, HD).transpose(0, 2, 1, 3).reshape(RECS, FRAMES, D)

def head_probs(query_head, key_head):
    scores = jnp.dot(query_head, key_head.T, preferred_element_type=jnp.float32) * HD ** (-0.5)
    shifted = jnp.exp(scores - lax.optimization_barrier(jnp.max(scores, axis=1, keepdims=True)))
    return shifted / lax.optimization_barrier(jnp.sum(shifted, axis=1, keepdims=True))

def attend_forward(operands):
    query_head, key_head, value_head = operands
    rounded = head_probs(query_head, key_head).astype(jnp.bfloat16)
    return jnp.dot(rounded, value_head, preferred_element_type=jnp.float32).astype(jnp.bfloat16)

def attend_backward(operands):
    query_head, key_head, value_head, grad_head, context_head = operands
    scaling = HD ** (-0.5)
    probabilities = head_probs(query_head, key_head)
    rounded = probabilities.astype(jnp.bfloat16)
    row_dots = lax.optimization_barrier(jnp.sum(grad_head.astype(jnp.float32) * context_head.astype(jnp.float32), axis=1, keepdims=True))
    prob_grad = jnp.dot(grad_head, value_head.T, preferred_element_type=jnp.float32)
    score_grad = (probabilities * (prob_grad - row_dots) * scaling).astype(jnp.bfloat16)
    query_grad = jnp.dot(score_grad, key_head, preferred_element_type=jnp.float32).astype(jnp.bfloat16)
    key_grad = jnp.dot(score_grad.T, query_head, preferred_element_type=jnp.float32).astype(jnp.bfloat16)
    value_grad = jnp.dot(rounded.T, grad_head, preferred_element_type=jnp.float32).astype(jnp.bfloat16)
    return (query_grad, key_grad, value_grad)

def reference(queries, key_vecs, value_vecs, residual_in, point_weight, context_grad, depth_kernel, norm_gain, norm_bias, conv_grad):
    query_split = to_heads(queries)
    key_split = to_heads(key_vecs)
    value_split = to_heads(value_vecs)
    context_split = lax.map(attend_forward, (query_split, key_split, value_split))
    context = from_heads(context_split)
    mixed = (residual_in.astype(jnp.float32) + context.astype(jnp.float32)).astype(jnp.bfloat16)
    conv_input = jnp.dot(mixed.reshape(RECS * FRAMES, D), point_weight, preferred_element_type=jnp.float32).astype(jnp.bfloat16).reshape(RECS, FRAMES, 2 * D)
    span = KERNEL - 1
    value_half = conv_input[:, :, :D].astype(jnp.float32)
    gate_sig = jax.nn.sigmoid(conv_input[:, :, D:].astype(jnp.float32))
    glu = (value_half * gate_sig).astype(jnp.bfloat16)
    glu_view = lax.optimization_barrier(glu).astype(jnp.float32)
    glu_wide = jnp.pad(glu_view, ((0, 0), (span, 0), (0, 0)))
    depthwise = jnp.zeros((RECS, FRAMES, D), jnp.float32)
    for offset in range(KERNEL):
        depthwise = depthwise + depth_kernel[offset] * glu_wide[:, offset:offset + FRAMES]
    average = lax.optimization_barrier(jnp.mean(depthwise, axis=2, keepdims=True))
    centered = depthwise - average
    variance = lax.optimization_barrier(jnp.mean(centered * centered, axis=2, keepdims=True))
    inverse = lax.rsqrt(variance + 1e-05)
    normed = centered * inverse
    affine = normed * norm_gain + norm_bias
    sig_affine = jax.nn.sigmoid(affine)
    conv_output = (affine * sig_affine).astype(jnp.bfloat16)
    affine_grad = conv_grad.astype(jnp.float32) * (sig_affine * (1.0 + affine * (1.0 - sig_affine)))
    gain_grad = lax.optimization_barrier(jnp.sum(affine_grad * normed, axis=(0, 1))) / RECS
    bias_grad = lax.optimization_barrier(jnp.sum(affine_grad, axis=(0, 1))) / RECS
    normed_grad = affine_grad * norm_gain
    depth_grad = inverse * (normed_grad - lax.optimization_barrier(jnp.mean(normed_grad, axis=2, keepdims=True)) - normed * lax.optimization_barrier(jnp.mean(normed_grad * normed, axis=2, keepdims=True)))
    kernel_grad = jnp.stack([lax.optimization_barrier(jnp.sum(depth_grad * glu_wide[:, offset:offset + FRAMES], axis=(0, 1))) for offset in range(KERNEL)]) / RECS
    grad_wide = jnp.pad(depth_grad, ((0, 0), (0, span), (0, 0)))
    glu_grad = jnp.zeros((RECS, FRAMES, D), jnp.float32)
    for offset in range(KERNEL):
        begin = span - offset
        glu_grad = glu_grad + depth_kernel[offset] * grad_wide[:, begin:begin + FRAMES]
    input_grad = jnp.concatenate([glu_grad * gate_sig, glu_grad * value_half * gate_sig * (1.0 - gate_sig)], axis=2).astype(jnp.bfloat16)
    mixed_grad = jnp.dot(input_grad.reshape(RECS * FRAMES, 2 * D), point_weight.T, preferred_element_type=jnp.float32).reshape(RECS, FRAMES, D)
    residual_grad = (context_grad.astype(jnp.float32) + mixed_grad).astype(jnp.bfloat16)
    grads = lax.map(attend_backward, (query_split, key_split, value_split, to_heads(residual_grad), context_split))
    query_grad = from_heads(grads[0])
    key_grad = from_heads(grads[1])
    value_grad = from_heads(grads[2])
    return (context, conv_output, query_grad, key_grad, value_grad, input_grad, residual_grad, kernel_grad, gain_grad, bias_grad)
```

```python
import functools
import jax
import jax.numpy as jnp
from jax import lax
from jax.sharding import PartitionSpec as P
from jax.experimental import pallas as pl
from jax.experimental.pallas import tpu as pltpu

HEADS = 16


def from_behind(block, axis, distance):
    devices = range(lax.axis_size(axis))
    route = [(i - distance, i) for i in devices if i - distance in devices]
    return lax.ppermute(block, axis, route)


def block_probs(query_block, key_heads, scaling):
    scores = (
        jnp.einsum("qhd,khd->hqk", query_block, key_heads, preferred_element_type=jnp.float32)
        * scaling
    )
    shifted = jnp.exp(scores - jnp.max(scores, axis=2, keepdims=True))
    return shifted / jnp.sum(shifted, axis=2, keepdims=True)


def attend_forward(query_part, key_part, value_part, head_count):
    frames, channels = query_part.shape
    head_depth = channels // head_count
    scaling = head_depth ** (-0.5)
    query_heads = query_part.reshape(frames, head_count, head_depth)
    key_heads = key_part.reshape(frames, head_count, head_depth)
    value_heads = value_part.reshape(frames, head_count, head_depth)
    block_rows = min(512, frames)

    def one_block(running, index):
        query_block = lax.dynamic_slice_in_dim(query_heads, index * block_rows, block_rows, 0)
        rounded = block_probs(query_block, key_heads, scaling).astype(jnp.bfloat16)
        context = jnp.einsum(
            "hqk,khd->qhd", rounded, value_heads, preferred_element_type=jnp.float32
        ).astype(jnp.bfloat16)
        return (running, context)

    unused, blocks = lax.scan(
        one_block, jnp.zeros((), jnp.float32), jnp.arange(frames // block_rows)
    )
    return blocks.reshape(frames, channels)


def attend_backward(query_part, key_part, value_part, grad_part, context_part, head_count):
    frames, channels = query_part.shape
    head_depth = channels // head_count
    scaling = head_depth ** (-0.5)
    query_heads = query_part.reshape(frames, head_count, head_depth)
    key_heads = key_part.reshape(frames, head_count, head_depth)
    value_heads = value_part.reshape(frames, head_count, head_depth)
    grad_heads = grad_part.reshape(frames, head_count, head_depth)
    context_heads = context_part.reshape(frames, head_count, head_depth)
    block_rows = min(512, frames)

    def one_block(running, index):
        key_total, value_total = running
        start = index * block_rows
        query_block = lax.dynamic_slice_in_dim(query_heads, start, block_rows, 0)
        grad_block = lax.dynamic_slice_in_dim(grad_heads, start, block_rows, 0)
        context_block = lax.dynamic_slice_in_dim(context_heads, start, block_rows, 0)
        probabilities = block_probs(query_block, key_heads, scaling)
        rounded = probabilities.astype(jnp.bfloat16)
        row_dots = jnp.sum(
            grad_block.astype(jnp.float32) * context_block.astype(jnp.float32), axis=2
        )
        prob_grad = jnp.einsum(
            "qhd,khd->hqk", grad_block, value_heads, preferred_element_type=jnp.float32
        )
        score_grad = (probabilities * (prob_grad - row_dots.T[:, :, None]) * scaling).astype(
            jnp.bfloat16
        )
        query_grad = jnp.einsum(
            "hqk,khd->qhd", score_grad, key_heads, preferred_element_type=jnp.float32
        ).astype(jnp.bfloat16)
        key_total = key_total + jnp.einsum(
            "hqk,qhd->khd", score_grad, query_block, preferred_element_type=jnp.float32
        )
        value_total = value_total + jnp.einsum(
            "hqk,qhd->khd", rounded, grad_block, preferred_element_type=jnp.float32
        )
        return ((key_total, value_total), query_grad)

    empty = jnp.zeros((frames, head_count, head_depth), jnp.float32)
    totals, blocks = lax.scan(one_block, (empty, empty), jnp.arange(frames // block_rows))
    query_grad = blocks.reshape(frames, channels)
    key_grad = totals[0].astype(jnp.bfloat16).reshape(frames, channels)
    value_grad = totals[1].astype(jnp.bfloat16).reshape(frames, channels)
    return (query_grad, key_grad, value_grad)


def shards(
    queries,
    key_vecs,
    value_vecs,
    residual_in,
    point_weight,
    context_grad,
    depth_kernel,
    norm_gain,
    norm_bias,
    conv_grad,
):
    head_count = HEADS // lax.axis_size("seq")
    query_heads, key_heads, value_heads = (
        lax.all_to_all(queries, "seq", split_axis=2, concat_axis=1, tiled=True),
        lax.all_to_all(key_vecs, "seq", split_axis=2, concat_axis=1, tiled=True),
        lax.all_to_all(value_vecs, "seq", split_axis=2, concat_axis=1, tiled=True),
    )
    context_local = attend_forward(query_heads[0], key_heads[0], value_heads[0], head_count)
    context_out = lax.all_to_all(
        context_local[None], "seq", split_axis=1, concat_axis=2, tiled=True
    )
    taps = depth_kernel.shape[0]
    channels = depth_kernel.shape[1]
    span = taps - 1
    frames = residual_in.shape[1]
    mixed = (residual_in[0].astype(jnp.float32) + context_out[0].astype(jnp.float32)).astype(
        jnp.bfloat16
    )
    pre_conv = jnp.dot(
        mixed,
        lax.all_gather(point_weight, "seq", axis=0, tiled=True),
        preferred_element_type=jnp.float32,
    )
    conv_input = pre_conv.astype(jnp.bfloat16)[None]
    value_half = conv_input[:, :, :channels].astype(jnp.float32)
    gate_sig = jax.nn.sigmoid(conv_input[:, :, channels:].astype(jnp.float32))
    glu = (value_half * gate_sig).astype(jnp.bfloat16)
    earlier = from_behind(glu[:, frames - span :], "seq", 1)
    glu_wide = jnp.concatenate([earlier, glu], axis=1)
    glu_view = lax.optimization_barrier(glu_wide).astype(jnp.float32)
    depthwise = jnp.zeros((1, frames, channels), jnp.float32)
    for offset in range(taps):
        depthwise = depthwise + depth_kernel[offset] * glu_view[:, offset : offset + frames]
    average = jnp.mean(depthwise, axis=2, keepdims=True)
    centered = depthwise - average
    variance = jnp.mean(centered * centered, axis=2, keepdims=True)
    inverse = lax.rsqrt(variance + 1e-05)
    normed = centered * inverse
    affine = normed * norm_gain + norm_bias
    sig_affine = jax.nn.sigmoid(affine)
    conv_output = (affine * sig_affine).astype(jnp.bfloat16)
    affine_grad = conv_grad.astype(jnp.float32) * (sig_affine * (1.0 + affine * (1.0 - sig_affine)))
    gain_term = jnp.sum(affine_grad * normed, axis=(0, 1))
    bias_term = jnp.sum(affine_grad, axis=(0, 1))
    normed_grad = affine_grad * norm_gain
    depth_grad = inverse * (
        normed_grad
        - jnp.mean(normed_grad, axis=2, keepdims=True)
        - normed * jnp.mean(normed_grad * normed, axis=2, keepdims=True)
    )
    kernel_term = jnp.stack(
        [
            jnp.sum(depth_grad * glu_view[:, offset : offset + frames], axis=(0, 1))
            for offset in range(taps)
        ]
    )
    kernel_total, gain_total, bias_total = lax.psum(
        (kernel_term, gain_term, bias_term), ("dp", "seq")
    )
    recordings = lax.axis_size("dp")
    kernel_grad = kernel_total / recordings
    gain_grad = gain_total / recordings
    bias_grad = bias_total / recordings
    later = from_behind(depth_grad[:, :span], "seq", -1)
    grad_wide = jnp.concatenate([depth_grad, later], axis=1)
    glu_grad = jnp.zeros((1, frames, channels), jnp.float32)
    for offset in range(taps):
        begin = span - offset
        glu_grad = glu_grad + depth_kernel[offset] * grad_wide[:, begin : begin + frames]
    input_grad = jnp.concatenate(
        [glu_grad * gate_sig, glu_grad * value_half * gate_sig * (1.0 - gate_sig)], axis=2
    ).astype(jnp.bfloat16)
    slope_rows = input_grad[0]
    mixed_grad = jnp.einsum(
        "fc,dc->fd",
        slope_rows,
        lax.all_gather(point_weight, "seq", axis=0, tiled=True),
        preferred_element_type=jnp.float32,
    )
    residual_grad = (context_grad.astype(jnp.float32) + mixed_grad[None]).astype(jnp.bfloat16)
    grad_heads = lax.all_to_all(residual_grad, "seq", split_axis=2, concat_axis=1, tiled=True)
    query_grad, key_grad, value_grad = attend_backward(
        query_heads[0], key_heads[0], value_heads[0], grad_heads[0], context_local, head_count
    )
    query_out, key_out, value_out = (
        lax.all_to_all(query_grad[None], "seq", split_axis=1, concat_axis=2, tiled=True),
        lax.all_to_all(key_grad[None], "seq", split_axis=1, concat_axis=2, tiled=True),
        lax.all_to_all(value_grad[None], "seq", split_axis=1, concat_axis=2, tiled=True),
    )
    return (
        context_out,
        conv_output,
        query_out,
        key_out,
        value_out,
        input_grad,
        residual_grad,
        kernel_grad,
        gain_grad,
        bias_grad,
    )


BF = jnp.bfloat16
F32 = jnp.float32
HALO = 32
LANES = 128
TERM_ROWS = 40


def fused_kernel(
    dims,
    q_ref, k_ref, v_ref, res_ref, w_ref, cg_ref, taps_ref, gain_ref, bias_ref, og_ref,
    ctx_out, conv_out, dq_out, dk_out, dv_out, ig_out, rg_out, kg_out, gg_out, bg_out,
    q_h, k_h, v_h, g_h, qt, kt, vt, gt, ctxt, ctx_h, prob, ds_s, pb_s, dqt, dq_h, dk_h, dv_h,
    w_full, mixed, a_s, sig_s, glu_f, dw, ng_s, dg, part, rs_buf, s2_buf, fin,
    ssem, rsem, lsem,
):
    n_seq, n_dp, rows, channels, taps, depth = dims
    own = channels // n_seq
    pairs = own // LANES
    frames = rows * n_seq
    chunks = channels // LANES
    scaling = depth ** (-0.5)
    me = lax.axis_index("seq")
    dp = lax.axis_index("dp")
    core = lax.rem(me, 2)
    mate = me + 1 - 2 * core
    across = lax.rem(me + 2, n_seq)
    x_pos = lax.rem(dp, 2)
    x_dp = dp + 1 - 2 * x_pos
    counter = [0]

    def remote(src, dst, device):
        index = counter[0]
        counter[0] += 1
        return pltpu.make_async_remote_copy(
            src_ref=src, dst_ref=dst, send_sem=ssem.at[index], recv_sem=rsem.at[index],
            device_id=device, device_id_type=pl.DeviceIdType.MESH,
        )

    peers = [lax.rem(me + d, n_seq) for d in range(1, n_seq)]
    dp_peers = [lax.rem(dp + d, n_dp) for d in range(1, n_dp)]
    barrier = pltpu.get_barrier_semaphore()
    for p in peers:
        pl.semaphore_signal(barrier, inc=1, device_id=(dp, p), device_id_type=pl.DeviceIdType.MESH)
    for p in dp_peers:
        pl.semaphore_signal(barrier, inc=1, device_id=(p, me), device_id_type=pl.DeviceIdType.MESH)
    pl.semaphore_wait(barrier, n_seq - 1 + n_dp - 1)

    pending = []

    def at(value, size):
        return pl.ds(pl.multiple_of(value * size, size), size)

    def scatter_heads(src, dst):
        copies = []
        for p in peers:
            copy = remote(src.at[:, at(p, own)], dst.at[at(me, rows), :], (dp, p))
            copy.start()
            copies.append(copy)
        return copies

    sends = []
    local = []
    for t, (src, dst) in enumerate(((q_ref, q_h), (k_ref, k_h), (v_ref, v_h))):
        sends.append(scatter_heads(src, dst))
        copy = pltpu.make_async_copy(src.at[:, at(me, own)], dst.at[at(me, rows), :], lsem.at[t])
        copy.start()
        local.append(copy)

    w_rows = w_ref.shape[0]
    half = w_rows // 2
    pieces = 2
    piece = half // pieces
    w_mate = remote(w_ref, w_full.at[at(me, w_rows), :], (dp, mate))
    w_mate.start()
    w_self = pltpu.make_async_copy(w_ref, w_full.at[at(me, w_rows), :], lsem.at[3])
    w_self.start()
    w_across = []
    for j in range(pieces):
        start = pl.multiple_of(x_pos * half + j * piece, piece)
        copy = remote(
            w_ref.at[pl.ds(start, piece), :],
            w_full.at[pl.ds(pl.multiple_of(me * w_rows + start, piece), piece), :],
            (dp, across),
        )
        copy.start()
        w_across.append(copy)

    def flip(ref):
        return ref[...].astype(F32).T

    def arrive(t):
        local[t].wait()
        for copy in sends[t]:
            copy.wait_recv()

    arrive(0)
    qt[...] = (flip(q_h) * scaling).astype(BF)
    arrive(1)
    kt[...] = flip(k_h).astype(BF)
    arrive(2)
    vt[...] = flip(v_h).astype(BF)

    q_block = min(256, frames)

    def forward_head(h):
        hr = slice(h * depth, (h + 1) * depth)

        def body(b, carry):
            cols = at(b, q_block)
            scores = jnp.dot(k_h[:, hr], qt[hr, cols], preferred_element_type=F32)
            shifted = jnp.exp(scores - jnp.max(scores, axis=0, keepdims=True))
            p = shifted * (1.0 / jnp.sum(shifted, axis=0, keepdims=True))
            prob[h, :, cols] = p
            ctxt[hr, cols] = jnp.dot(vt[hr, :], p.astype(BF), preferred_element_type=F32).astype(BF)
            return carry

        lax.fori_loop(0, frames // q_block, body, 0)

    def gather_pair(src, dst, pair, t):
        copies = []
        width = LANES
        target = pl.ds(pl.multiple_of(me * own + pair * width, width), width)
        source = slice(pair * width, (pair + 1) * width)
        for p in peers:
            copy = remote(src.at[at(p, rows), source], dst.at[:, target], (dp, p))
            copy.start()
            copies.append(copy)
        keep = pltpu.make_async_copy(src.at[at(me, rows), source], dst.at[:, target], lsem.at[t])
        keep.start()
        return copies, keep

    ctx_copies = []
    for pair in range(pairs):
        forward_head(2 * pair)
        forward_head(2 * pair + 1)
        pc = slice(pair * LANES, (pair + 1) * LANES)
        ctx_h[:, pc] = ctxt[pc, :].astype(F32).T.astype(BF)
        ctx_copies.append(gather_pair(ctx_h, ctx_out, pair, 4 + pair))

    w_x, w_fwd1, w_fwd2 = [], [], []
    for j in range(pieces):
        w_across[j].wait_recv()
        here = pl.ds(pl.multiple_of(across * w_rows + x_pos * half + j * piece, piece), piece)
        copy = remote(w_full.at[here, :], w_full.at[here, :], (x_dp, me))
        copy.start()
        w_x.append(copy)
        copy = remote(w_full.at[here, :], w_full.at[here, :], (dp, mate))
        copy.start()
        w_fwd1.append(copy)
    for j in range(pieces):
        w_x[j].wait_recv()
        here = pl.ds(
            pl.multiple_of(across * w_rows + (1 - x_pos) * half + j * piece, piece), piece
        )
        copy = remote(w_full.at[here, :], w_full.at[here, :], (dp, mate))
        copy.start()
        w_fwd2.append(copy)

    for copies, keep in ctx_copies:
        keep.wait()
        for copy in copies:
            copy.wait_recv()
    mixed[...] = (res_ref[...].astype(F32) + ctx_out[...].astype(F32)).astype(BF)
    w_self.wait()
    w_mate.wait_recv()
    for copy in w_fwd1 + w_fwd2:
        copy.wait_recv()

    wide = 2 * LANES

    def conv_in(i, carry):
        cols = at(i, wide)
        gates = pl.ds(pl.multiple_of(channels + i * wide, wide), wide)
        a = jnp.dot(mixed[...], w_full[:, cols], preferred_element_type=F32).astype(BF)
        b = jnp.dot(mixed[...], w_full[:, gates], preferred_element_type=F32).astype(BF)
        sig = jax.nn.sigmoid(b.astype(F32))
        a_s[:, cols] = a
        sig_s[:, cols] = sig
        glu = (a.astype(F32) * sig).astype(BF).astype(F32)
        glu_f[2 * i, HALO : HALO + rows, :] = glu[:, :LANES]
        glu_f[2 * i + 1, HALO : HALO + rows, :] = glu[:, LANES:]
        return carry

    lax.fori_loop(0, channels // wide, conv_in, 0)
    halo1 = remote(
        glu_f.at[:, rows : rows + HALO, :], glu_f.at[:, 0:HALO, :], (dp, lax.rem(me + 1, n_seq))
    )
    halo1.start()
    halo1.wait_recv()
    halo1.wait_send()

    @pl.when(me == 0)
    def _():
        glu_f[:, 0:HALO, :] = jnp.zeros((chunks, HALO, LANES), F32)

    span = taps - 1
    base = HALO - span

    def depth_conv(c, total):
        lanes = at(c, LANES)
        acc = jnp.zeros((rows, LANES), F32)
        for o in range(taps):
            acc = acc + taps_ref[o : o + 1, lanes] * glu_f[c, base + o : base + o + rows, :]
        dw[c] = acc
        return total + acc

    zero = jnp.zeros((rows, LANES), F32)
    total = lax.fori_loop(0, chunks, depth_conv, zero)
    average = jnp.sum(total, axis=1, keepdims=True) * (1.0 / channels)

    def squares(c, total):
        centered = dw[c] - average
        return total + centered * centered

    total = lax.fori_loop(0, chunks, squares, zero)
    variance = jnp.sum(total, axis=1, keepdims=True) * (1.0 / channels)
    inverse = lax.rsqrt(variance + 1e-05)

    def norm_step(c, carry):
        s1, s2 = carry
        lanes = at(c, LANES)
        normed = (dw[c] - average) * inverse
        affine = normed * gain_ref[:, lanes] + bias_ref[:, lanes]
        sig = jax.nn.sigmoid(affine)
        conv_out[:, lanes] = (affine * sig).astype(BF)
        affine_grad = og_ref[:, lanes].astype(F32) * (sig * (1.0 + affine * (1.0 - sig)))
        part[c, taps : taps + 1, :] = jnp.sum(affine_grad * normed, axis=0, keepdims=True)
        part[c, taps + 1 : taps + 2, :] = jnp.sum(affine_grad, axis=0, keepdims=True)
        normed_grad = affine_grad * gain_ref[:, lanes]
        dw[c] = normed
        ng_s[c] = normed_grad
        return s1 + normed_grad, s2 + normed_grad * normed

    s1, s2 = lax.fori_loop(0, chunks, norm_step, (zero, zero))
    m1 = jnp.sum(s1, axis=1, keepdims=True) * (1.0 / channels)
    m2 = jnp.sum(s2, axis=1, keepdims=True) * (1.0 / channels)

    def depth_grad_step(c, carry):
        dg[c, 0:rows, :] = inverse * (ng_s[c] - m1 - dw[c] * m2)
        return carry

    lax.fori_loop(0, chunks, depth_grad_step, 0)
    halo2 = remote(
        dg.at[:, 0:HALO, :], dg.at[:, rows : rows + HALO, :], (dp, lax.rem(me + n_seq - 1, n_seq))
    )
    halo2.start()

    def tap_grad(c, carry):
        grad = dg[c, 0:rows, :]
        for o in range(taps):
            part[c, o : o + 1, :] = jnp.sum(
                grad * glu_f[c, base + o : base + o + rows, :], axis=0, keepdims=True
            )
        part[c, taps + 2 : TERM_ROWS, :] = jnp.zeros((TERM_ROWS - taps - 2, LANES), F32)
        return carry

    lax.fori_loop(0, chunks, tap_grad, 0)
    reduce1 = []
    for d, p in enumerate(dp_peers):
        copy = remote(part.at[p], rs_buf.at[d], (p, me))
        copy.start()
        reduce1.append(copy)

    halo2.wait_recv()
    halo2.wait_send()

    @pl.when(me == n_seq - 1)
    def _():
        dg[:, rows : rows + HALO, :] = jnp.zeros((chunks, HALO, LANES), F32)

    def glu_back(c, carry):
        lanes = at(c, LANES)
        gates = pl.ds(pl.multiple_of(channels + c * LANES, LANES), LANES)
        acc = jnp.zeros((rows, LANES), F32)
        for o in range(taps):
            acc = acc + taps_ref[o : o + 1, lanes] * dg[c, span - o : span - o + rows, :]
        sig = sig_s[:, lanes]
        ig_out[:, lanes] = (acc * sig).astype(BF)
        ig_out[:, gates] = (acc * a_s[:, lanes].astype(F32) * sig * (1.0 - sig)).astype(BF)
        return carry

    lax.fori_loop(0, chunks, glu_back, 0)

    def mixed_back(i, carry):
        cols = at(i, wide)
        grad = lax.dot_general(
            ig_out[...], w_full[cols, :], (((1,), (1,)), ((), ())), preferred_element_type=F32
        )
        rg_out[:, cols] = (cg_ref[:, cols].astype(F32) + grad).astype(BF)
        return carry

    lax.fori_loop(0, channels // wide, mixed_back, 0)
    g_send = scatter_heads(rg_out, g_h)
    g_self = pltpu.make_async_copy(
        rg_out.at[:, at(me, own)], g_h.at[at(me, rows), :], lsem.at[6]
    )
    g_self.start()

    for copy in reduce1:
        copy.wait_recv()
    total = part[dp]
    for d in range(n_dp - 1):
        total = total + rs_buf[d]
    s2_buf[me] = total
    reduce2 = []
    for p in peers:
        copy = remote(s2_buf.at[me], s2_buf.at[me], (dp, p))
        copy.start()
        reduce2.append(copy)

    g_self.wait()
    for copy in g_send:
        copy.wait_recv()
    gt[...] = flip(g_h).astype(BF)

    def backward_head(h):
        hr = slice(h * depth, (h + 1) * depth)
        slot = h % 2

        def body(b, carry):
            cols = at(b, q_block)
            grad = gt[hr, cols]
            dots = jnp.sum(
                grad.astype(F32) * ctxt[hr, cols].astype(F32), axis=0, keepdims=True
            )
            prob_grad = jnp.dot(v_h[:, hr], grad, preferred_element_type=F32)
            p = prob[h, :, cols]
            score_grad = (p * (prob_grad - dots) * scaling).astype(BF)
            pb_s[slot, :, cols] = p.astype(BF)
            ds_s[slot, :, cols] = score_grad
            dqt[hr, cols] = jnp.dot(kt[hr, :], score_grad, preferred_element_type=F32)
            return carry

        lax.fori_loop(0, frames // q_block, body, 0)

    first = lax.broadcasted_iota(jnp.int32, (frames, LANES), 1) < depth
    out_copies = []
    reduce3 = []
    for pair in range(pairs):
        pc = slice(pair * LANES, (pair + 1) * LANES)
        backward_head(2 * pair)
        backward_head(2 * pair + 1)
        dq_h[:, pc] = dqt[pc, :].T.astype(BF)
        out_copies.append(gather_pair(dq_h, dq_out, pair, 7 + 3 * pair))
        left = jnp.dot(ds_s[0], q_h[:, pc], preferred_element_type=F32)
        right = jnp.dot(ds_s[1], q_h[:, pc], preferred_element_type=F32)
        dk_h[:, pc] = jnp.where(first, left, right).astype(BF)
        out_copies.append(gather_pair(dk_h, dk_out, pair, 8 + 3 * pair))
        left = jnp.dot(pb_s[0], g_h[:, pc], preferred_element_type=F32)
        right = jnp.dot(pb_s[1], g_h[:, pc], preferred_element_type=F32)
        dv_h[:, pc] = jnp.where(first, left, right).astype(BF)
        out_copies.append(gather_pair(dv_h, dv_out, pair, 9 + 3 * pair))
        if pair == 0:
            for copy in reduce2:
                copy.wait_recv()
            total = s2_buf[0]
            for s in range(1, n_seq):
                total = total + s2_buf[s]
            fin[dp] = total * (1.0 / n_dp)
            for p in dp_peers:
                copy = remote(fin.at[dp], fin.at[dp], (p, me))
                copy.start()
                reduce3.append(copy)

    for copy in reduce3:
        copy.wait_recv()
    for c in range(chunks):
        lanes = slice(c * LANES, (c + 1) * LANES)
        kg_out[:, lanes] = fin[c, 0:taps, :]
        gg_out[:, lanes] = fin[c, taps : taps + 1, :]
        bg_out[:, lanes] = fin[c, taps + 1 : taps + 2, :]

    for copies, keep in out_copies:
        keep.wait()
        for copy in copies:
            copy.wait_recv()
    for copies in sends + [c for c, _ in ctx_copies] + [c for c, _ in out_copies]:
        for copy in copies:
            copy.wait_send()
    for copy in (
        [w_mate] + w_across + w_x + w_fwd1 + w_fwd2 + g_send + reduce1 + reduce2 + reduce3
    ):
        copy.wait_send()


def fused_shards(
    queries, key_vecs, value_vecs, residual_in, point_weight, context_grad, depth_kernel,
    norm_gain, norm_bias, conv_grad,
):
    n_seq = lax.axis_size("seq")
    n_dp = lax.axis_size("dp")
    rows, channels = queries.shape[1:]
    taps = depth_kernel.shape[0]
    depth = channels // HEADS
    frames = rows * n_seq
    own = channels // n_seq
    heads = own // depth
    chunks = channels // LANES
    s = jax.ShapeDtypeStruct
    vm = pltpu.VMEM
    block = s((rows, channels), BF)
    head_rows = vm((frames, own), BF)
    head_cols = vm((own, frames), BF)
    n_copies = 96
    scratch = (
        [head_rows] * 4 + [head_cols] * 5 + [head_rows]
        + [vm((heads, frames, frames), F32), vm((2, frames, frames), BF), vm((2, frames, frames), BF)]
        + [vm((own, frames), F32)] + [head_rows] * 3
        + [
            vm((channels, 2 * channels), BF),
            vm((rows, channels), BF),
            vm((rows, channels), BF),
            vm((rows, channels), F32),
            vm((chunks, HALO + rows, LANES), F32),
            vm((chunks, rows, LANES), F32),
            vm((chunks, rows, LANES), F32),
            vm((chunks, rows + HALO, LANES), F32),
            vm((chunks, TERM_ROWS, LANES), F32),
            vm((n_dp - 1, TERM_ROWS, LANES), F32),
            vm((n_seq, TERM_ROWS, LANES), F32),
            vm((chunks, TERM_ROWS, LANES), F32),
            pltpu.SemaphoreType.DMA((n_copies,)),
            pltpu.SemaphoreType.DMA((n_copies,)),
            pltpu.SemaphoreType.DMA((16,)),
        ]
    )
    spec = pl.BlockSpec(memory_space=pltpu.VMEM)
    outs = pl.pallas_call(
        functools.partial(fused_kernel, (n_seq, n_dp, rows, channels, taps, depth)),
        out_shape=(
            block, block, block, block, block, s((rows, 2 * channels), BF), block,
            s((taps, channels), F32), s((1, channels), F32), s((1, channels), F32),
        ),
        in_specs=[spec] * 10,
        out_specs=(spec,) * 10,
        scratch_shapes=scratch,
        compiler_params=pltpu.CompilerParams(
            collective_id=0, has_side_effects=True, vmem_limit_bytes=56 * 1024 * 1024
        ),
    )(
        queries[0], key_vecs[0], value_vecs[0], residual_in[0], point_weight, context_grad[0],
        depth_kernel, norm_gain[None], norm_bias[None], conv_grad[0],
    )
    return tuple(o[None] for o in outs[:7]) + (outs[7], outs[8][0], outs[9][0])


def chosen(*args):
    n_seq = lax.axis_size("seq")
    n_dp = lax.axis_size("dp")
    recs, rows, channels = args[0].shape
    fits = (
        n_seq == 4
        and recs == 1
        and rows % 128 == 0
        and channels % (LANES * n_seq) == 0
        and 2 * channels == LANES * HEADS
        and channels // LANES == n_dp
        and rows * n_seq <= 512
        and args[6].shape[0] <= 32
    )
    return fused_shards(*args) if fits else shards(*args)


def solution(mesh):
    in_specs = (
        P("dp", "seq", None),
        P("dp", "seq", None),
        P("dp", "seq", None),
        P("dp", "seq", None),
        P("seq", None),
        P("dp", "seq", None),
        P(),
        P(),
        P(),
        P("dp", "seq", None),
    )
    out_specs = (
        P("dp", "seq", None),
        P("dp", "seq", None),
        P("dp", "seq", None),
        P("dp", "seq", None),
        P("dp", "seq", None),
        P("dp", "seq", None),
        P("dp", "seq", None),
        P(),
        P(),
        P(),
    )
    return jax.shard_map(chosen, mesh=mesh, in_specs=in_specs, out_specs=out_specs, check_vma=False)
```

```python
import functools
import jax
import jax.numpy as jnp
from jax import lax
from jax.sharding import PartitionSpec as P
from jax.experimental import pallas as pl
from jax.experimental.pallas import tpu as pltpu

HEADS = 16


def from_behind(block, axis, distance):
    devices = range(lax.axis_size(axis))
    route = [(i - distance, i) for i in devices if i - distance in devices]
    return lax.ppermute(block, axis, route)


def block_probs(query_block, key_heads, scaling):
    scores = (
        jnp.einsum("qhd,khd->hqk", query_block, key_heads, preferred_element_type=jnp.float32)
        * scaling
    )
    shifted = jnp.exp(scores - jnp.max(scores, axis=2, keepdims=True))
    return shifted / jnp.sum(shifted, axis=2, keepdims=True)


def attend_forward(query_part, key_part, value_part, head_count):
    frames, channels = query_part.shape
    head_depth = channels // head_count
    scaling = head_depth ** (-0.5)
    query_heads = query_part.reshape(frames, head_count, head_depth)
    key_heads = key_part.reshape(frames, head_count, head_depth)
    value_heads = value_part.reshape(frames, head_count, head_depth)
    block_rows = min(512, frames)

    def one_block(running, index):
        query_block = lax.dynamic_slice_in_dim(query_heads, index * block_rows, block_rows, 0)
        rounded = block_probs(query_block, key_heads, scaling).astype(jnp.bfloat16)
        context = jnp.einsum(
            "hqk,khd->qhd", rounded, value_heads, preferred_element_type=jnp.float32
        ).astype(jnp.bfloat16)
        return (running, context)

    unused, blocks = lax.scan(
        one_block, jnp.zeros((), jnp.float32), jnp.arange(frames // block_rows)
    )
    return blocks.reshape(frames, channels)


def attend_backward(query_part, key_part, value_part, grad_part, context_part, head_count):
    frames, channels = query_part.shape
    head_depth = channels // head_count
    scaling = head_depth ** (-0.5)
    query_heads = query_part.reshape(frames, head_count, head_depth)
    key_heads = key_part.reshape(frames, head_count, head_depth)
    value_heads = value_part.reshape(frames, head_count, head_depth)
    grad_heads = grad_part.reshape(frames, head_count, head_depth)
    context_heads = context_part.reshape(frames, head_count, head_depth)
    block_rows = min(512, frames)

    def one_block(running, index):
        key_total, value_total = running
        start = index * block_rows
        query_block = lax.dynamic_slice_in_dim(query_heads, start, block_rows, 0)
        grad_block = lax.dynamic_slice_in_dim(grad_heads, start, block_rows, 0)
        context_block = lax.dynamic_slice_in_dim(context_heads, start, block_rows, 0)
        probabilities = block_probs(query_block, key_heads, scaling)
        rounded = probabilities.astype(jnp.bfloat16)
        row_dots = jnp.sum(
            grad_block.astype(jnp.float32) * context_block.astype(jnp.float32), axis=2
        )
        prob_grad = jnp.einsum(
            "qhd,khd->hqk", grad_block, value_heads, preferred_element_type=jnp.float32
        )
        score_grad = (probabilities * (prob_grad - row_dots.T[:, :, None]) * scaling).astype(
            jnp.bfloat16
        )
        query_grad = jnp.einsum(
            "hqk,khd->qhd", score_grad, key_heads, preferred_element_type=jnp.float32
        ).astype(jnp.bfloat16)
        key_total = key_total + jnp.einsum(
            "hqk,qhd->khd", score_grad, query_block, preferred_element_type=jnp.float32
        )
        value_total = value_total + jnp.einsum(
            "hqk,qhd->khd", rounded, grad_block, preferred_element_type=jnp.float32
        )
        return ((key_total, value_total), query_grad)

    empty = jnp.zeros((frames, head_count, head_depth), jnp.float32)
    totals, blocks = lax.scan(one_block, (empty, empty), jnp.arange(frames // block_rows))
    query_grad = blocks.reshape(frames, channels)
    key_grad = totals[0].astype(jnp.bfloat16).reshape(frames, channels)
    value_grad = totals[1].astype(jnp.bfloat16).reshape(frames, channels)
    return (query_grad, key_grad, value_grad)


def shards(
    queries,
    key_vecs,
    value_vecs,
    residual_in,
    point_weight,
    context_grad,
    depth_kernel,
    norm_gain,
    norm_bias,
    conv_grad,
):
    head_count = HEADS // lax.axis_size("seq")
    query_heads, key_heads, value_heads = (
        lax.all_to_all(queries, "seq", split_axis=2, concat_axis=1, tiled=True),
        lax.all_to_all(key_vecs, "seq", split_axis=2, concat_axis=1, tiled=True),
        lax.all_to_all(value_vecs, "seq", split_axis=2, concat_axis=1, tiled=True),
    )
    context_local = attend_forward(query_heads[0], key_heads[0], value_heads[0], head_count)
    context_out = lax.all_to_all(
        context_local[None], "seq", split_axis=1, concat_axis=2, tiled=True
    )
    taps = depth_kernel.shape[0]
    channels = depth_kernel.shape[1]
    span = taps - 1
    frames = residual_in.shape[1]
    mixed = (residual_in[0].astype(jnp.float32) + context_out[0].astype(jnp.float32)).astype(
        jnp.bfloat16
    )
    pre_conv = jnp.dot(
        mixed,
        lax.all_gather(point_weight, "seq", axis=0, tiled=True),
        preferred_element_type=jnp.float32,
    )
    conv_input = pre_conv.astype(jnp.bfloat16)[None]
    value_half = conv_input[:, :, :channels].astype(jnp.float32)
    gate_sig = jax.nn.sigmoid(conv_input[:, :, channels:].astype(jnp.float32))
    glu = (value_half * gate_sig).astype(jnp.bfloat16)
    earlier = from_behind(glu[:, frames - span :], "seq", 1)
    glu_wide = jnp.concatenate([earlier, glu], axis=1)
    glu_view = lax.optimization_barrier(glu_wide).astype(jnp.float32)
    depthwise = jnp.zeros((1, frames, channels), jnp.float32)
    for offset in range(taps):
        depthwise = depthwise + depth_kernel[offset] * glu_view[:, offset : offset + frames]
    average = jnp.mean(depthwise, axis=2, keepdims=True)
    centered = depthwise - average
    variance = jnp.mean(centered * centered, axis=2, keepdims=True)
    inverse = lax.rsqrt(variance + 1e-05)
    normed = centered * inverse
    affine = normed * norm_gain + norm_bias
    sig_affine = jax.nn.sigmoid(affine)
    conv_output = (affine * sig_affine).astype(jnp.bfloat16)
    affine_grad = conv_grad.astype(jnp.float32) * (sig_affine * (1.0 + affine * (1.0 - sig_affine)))
    gain_term = jnp.sum(affine_grad * normed, axis=(0, 1))
    bias_term = jnp.sum(affine_grad, axis=(0, 1))
    normed_grad = affine_grad * norm_gain
    depth_grad = inverse * (
        normed_grad
        - jnp.mean(normed_grad, axis=2, keepdims=True)
        - normed * jnp.mean(normed_grad * normed, axis=2, keepdims=True)
    )
    kernel_term = jnp.stack(
        [
            jnp.sum(depth_grad * glu_view[:, offset : offset + frames], axis=(0, 1))
            for offset in range(taps)
        ]
    )
    kernel_total, gain_total, bias_total = lax.psum(
        (kernel_term, gain_term, bias_term), ("dp", "seq")
    )
    recordings = lax.axis_size("dp")
    kernel_grad = kernel_total / recordings
    gain_grad = gain_total / recordings
    bias_grad = bias_total / recordings
    later = from_behind(depth_grad[:, :span], "seq", -1)
    grad_wide = jnp.concatenate([depth_grad, later], axis=1)
    glu_grad = jnp.zeros((1, frames, channels), jnp.float32)
    for offset in range(taps):
        begin = span - offset
        glu_grad = glu_grad + depth_kernel[offset] * grad_wide[:, begin : begin + frames]
    input_grad = jnp.concatenate(
        [glu_grad * gate_sig, glu_grad * value_half * gate_sig * (1.0 - gate_sig)], axis=2
    ).astype(jnp.bfloat16)
    slope_rows = input_grad[0]
    mixed_grad = jnp.einsum(
        "fc,dc->fd",
        slope_rows,
        lax.all_gather(point_weight, "seq", axis=0, tiled=True),
        preferred_element_type=jnp.float32,
    )
    residual_grad = (context_grad.astype(jnp.float32) + mixed_grad[None]).astype(jnp.bfloat16)
    grad_heads = lax.all_to_all(residual_grad, "seq", split_axis=2, concat_axis=1, tiled=True)
    query_grad, key_grad, value_grad = attend_backward(
        query_heads[0], key_heads[0], value_heads[0], grad_heads[0], context_local, head_count
    )
    query_out, key_out, value_out = (
        lax.all_to_all(query_grad[None], "seq", split_axis=1, concat_axis=2, tiled=True),
        lax.all_to_all(key_grad[None], "seq", split_axis=1, concat_axis=2, tiled=True),
        lax.all_to_all(value_grad[None], "seq", split_axis=1, concat_axis=2, tiled=True),
    )
    return (
        context_out,
        conv_output,
        query_out,
        key_out,
        value_out,
        input_grad,
        residual_grad,
        kernel_grad,
        gain_grad,
        bias_grad,
    )


BF = jnp.bfloat16
F32 = jnp.float32
HALO = 32
LANES = 128
TERM_ROWS = 40


def fused_kernel(
    dims,
    q_ref, k_ref, v_ref, res_ref, w_ref, cg_ref, taps_ref, gain_ref, bias_ref, og_ref,
    ctx_out, conv_out, dq_out, dk_out, dv_out, ig_out, rg_out, kg_out, gg_out, bg_out,
    q_h, k_h, v_h, g_h, qt, kt, vt, gt, ctxt, ctx_h, prob, pb_s, ds_s, dqt, dq_h, dk_h, dv_h,
    res_v, cg_v, og_v, w_full, pre, mixed, a_s, sig_s, glu_f, dw, ng_s, dg, part, rs_buf, s2_buf, fin,
    ssem, rsem, lsem,
):
    n_seq, n_dp, rows, channels, taps, depth = dims
    own = channels // n_seq
    pairs = own // LANES
    frames = rows * n_seq
    chunks = channels // LANES
    scaling = depth ** (-0.5)
    me = lax.axis_index("seq")
    dp = lax.axis_index("dp")
    core = lax.rem(me, 2)
    mate = me + 1 - 2 * core
    across = lax.rem(me + 2, n_seq)
    x_pos = lax.rem(dp, 2)
    x_dp = dp + 1 - 2 * x_pos
    counter = [0]

    def remote(src, dst, device):
        index = counter[0]
        counter[0] += 1
        return pltpu.make_async_remote_copy(
            src_ref=src, dst_ref=dst, send_sem=ssem.at[index], recv_sem=rsem.at[index],
            device_id=device, device_id_type=pl.DeviceIdType.MESH,
        )

    diag = lax.rem(mate + 2, n_seq)
    chip = lax.div(me, 2)
    peers = [across, diag, mate]
    dp_peers = [lax.rem(dp + d, n_dp) for d in range(1, n_dp)]
    barrier = pltpu.get_barrier_semaphore()
    for p in peers:
        pl.semaphore_signal(barrier, inc=1, device_id=(dp, p), device_id_type=pl.DeviceIdType.MESH)
    for p in dp_peers:
        pl.semaphore_signal(barrier, inc=1, device_id=(p, me), device_id_type=pl.DeviceIdType.MESH)
    pl.semaphore_wait(barrier, n_seq - 1 + n_dp - 1)

    def at(value, size):
        return pl.ds(pl.multiple_of(value * size, size), size)

    loads = []
    for t, (src, dst) in enumerate(((res_ref, res_v), (cg_ref, cg_v), (og_ref, og_v))):
        copy = pltpu.make_async_copy(src, dst, lsem.at[t])
        copy.start()
        loads.append(copy)

    def head_cols(owner, pair):
        return pl.ds(pl.multiple_of(owner * own + pair * LANES, LANES), LANES)

    sends = []
    for pair in range(pairs):
        pc = slice(pair * LANES, (pair + 1) * LANES)
        for t, (src, dst) in enumerate(((q_ref, q_h), (k_ref, k_h), (v_ref, v_h))):
            copies = []
            for p in peers:
                copy = remote(src.at[:, head_cols(p, pair)], dst.at[at(me, rows), pc], (dp, p))
                copy.start()
                copies.append(copy)
            keep = pltpu.make_async_copy(
                src.at[:, head_cols(me, pair)], dst.at[at(me, rows), pc], lsem.at[4 + 3 * pair + t]
            )
            keep.start()
            sends.append((copies, keep))

    w_rows = w_ref.shape[0]
    half = w_rows // 2
    pieces = 2
    piece = half // pieces
    w_mate = remote(w_ref, w_full.at[at(me, w_rows), :], (dp, mate))
    w_mate.start()
    w_self = pltpu.make_async_copy(w_ref, w_full.at[at(me, w_rows), :], lsem.at[3])
    w_self.start()
    w_across = []
    for j in range(pieces):
        start = pl.multiple_of(x_pos * half + j * piece, piece)
        copy = remote(
            w_ref.at[pl.ds(start, piece), :],
            w_full.at[pl.ds(pl.multiple_of(me * w_rows + start, piece), piece), :],
            (dp, across),
        )
        copy.start()
        w_across.append(copy)

    def flip(value):
        return value.astype(F32).T

    def arrive(index):
        copies, keep = sends[index]
        keep.wait()
        for copy in copies:
            copy.wait_recv()

    q_block = min(256, frames)

    def forward_head(h):
        hr = slice(h * depth, (h + 1) * depth)

        def body(b, carry):
            cols = at(b, q_block)
            scores = jnp.dot(k_h[:, hr], qt[hr, cols], preferred_element_type=F32)
            shifted = jnp.exp(scores - jnp.max(scores, axis=0, keepdims=True))
            p = shifted * (1.0 / jnp.sum(shifted, axis=0, keepdims=True))
            rounded = p.astype(BF)
            prob[h, :, cols] = p
            pb_s[h, :, cols] = rounded
            ctxt[hr, cols] = jnp.dot(vt[hr, :], rounded, preferred_element_type=F32).astype(BF)
            return carry

        lax.fori_loop(0, frames // q_block, body, 0)

    def gather_pair(src, dst, pair, t):
        copies = []
        source = slice(pair * LANES, (pair + 1) * LANES)
        for p in peers:
            copy = remote(src.at[at(p, rows), source], dst.at[:, head_cols(me, pair)], (dp, p))
            copy.start()
            copies.append(copy)
        keep = pltpu.make_async_copy(
            src.at[at(me, rows), source], dst.at[:, head_cols(me, pair)], lsem.at[t]
        )
        keep.start()
        return copies, keep

    ctx_copies = []
    for pair in range(pairs):
        pc = slice(pair * LANES, (pair + 1) * LANES)
        arrive(3 * pair)
        qt[pc, :] = (flip(q_h[:, pc]) * scaling).astype(BF)
        arrive(3 * pair + 1)
        arrive(3 * pair + 2)
        vt[pc, :] = flip(v_h[:, pc]).astype(BF)
        forward_head(2 * pair)
        forward_head(2 * pair + 1)
        ctx_h[:, pc] = flip(ctxt[pc, :]).astype(BF)
        ctx_copies.append(gather_pair(ctx_h, ctx_out, pair, 10 + pair))

    def w_part(owner, side, j):
        return pl.ds(pl.multiple_of(owner * w_rows + side * half + j * piece, piece), piece)

    def forward(here, device):
        copy = remote(w_full.at[here, :], w_full.at[here, :], device)
        copy.start()
        return copy

    w_x, w_fwd = [], []
    for j in range(pieces):
        w_across[j].wait_recv()
        here = w_part(across, x_pos, j)
        w_x.append(forward(here, (x_dp, me)))
        w_fwd.append(forward(here, (dp, mate)))
        if j == 0:
            for pair in range(pairs):
                pc = slice(pair * LANES, (pair + 1) * LANES)
                kt[pc, :] = flip(k_h[:, pc]).astype(BF)

    for copies, keep in ctx_copies:
        keep.wait()
        copies[2].wait_recv()
    loads[0].wait()
    w_self.wait()
    w_mate.wait_recv()
    near = at(chip, 2 * own)
    far = at(1 - chip, 2 * own)
    wide = 2 * LANES
    mixed[:, near] = (res_v[:, near].astype(F32) + ctx_out[:, near].astype(F32)).astype(BF)

    def conv_near(i, carry):
        cols = at(i, wide)
        pre[:, cols] = jnp.dot(mixed[:, near], w_full[near, cols], preferred_element_type=F32)
        return carry

    lax.fori_loop(0, 2 * channels // wide, conv_near, 0)
    for j in range(pieces):
        w_x[j].wait_recv()
        w_fwd.append(forward(w_part(across, 1 - x_pos, j), (dp, mate)))
    for copies, keep in ctx_copies:
        copies[0].wait_recv()
        copies[1].wait_recv()
    mixed[:, far] = (res_v[:, far].astype(F32) + ctx_out[:, far].astype(F32)).astype(BF)
    for copy in w_fwd:
        copy.wait_recv()

    def conv_in(i, carry):
        cols = at(i, wide)
        gates = pl.ds(pl.multiple_of(channels + i * wide, wide), wide)
        a = jnp.dot(mixed[:, far], w_full[far, cols], preferred_element_type=F32)
        b = jnp.dot(mixed[:, far], w_full[far, gates], preferred_element_type=F32)
        a = (a + pre[:, cols]).astype(BF)
        b = (b + pre[:, gates]).astype(BF)
        sig = jax.nn.sigmoid(b.astype(F32))
        a_s[:, cols] = a
        sig_s[:, cols] = sig
        glu = (a.astype(F32) * sig).astype(BF).astype(F32)
        glu_f[2 * i, HALO : HALO + rows, :] = glu[:, :LANES]
        glu_f[2 * i + 1, HALO : HALO + rows, :] = glu[:, LANES:]
        return carry

    lax.fori_loop(0, channels // wide, conv_in, 0)
    halo1 = remote(
        glu_f.at[:, rows : rows + HALO, :], glu_f.at[:, 0:HALO, :], (dp, lax.rem(me + 1, n_seq))
    )
    halo1.start()
    span = taps - 1
    base = HALO - span

    def depth_rows(first, count):
        def body(c, total):
            lanes = at(c, LANES)
            acc = jnp.zeros((count, LANES), F32)
            for o in range(taps):
                low = base + first + o
                acc = acc + taps_ref[o : o + 1, lanes] * glu_f[c, low : low + count, :]
            dw[c, first : first + count, :] = acc
            return total + acc

        return lax.fori_loop(0, chunks, body, jnp.zeros((count, LANES), F32))

    total_late = depth_rows(HALO, rows - HALO)
    halo1.wait_recv()
    halo1.wait_send()

    @pl.when(me == 0)
    def _():
        glu_f[:, 0:HALO, :] = jnp.zeros((chunks, HALO, LANES), F32)

    total_early = depth_rows(0, HALO)
    average = jnp.concatenate(
        [jnp.sum(total_early, axis=1, keepdims=True), jnp.sum(total_late, axis=1, keepdims=True)],
        axis=0,
    ) * (1.0 / channels)
    zero = jnp.zeros((rows, LANES), F32)
    loads[2].wait()

    def squares(c, total):
        centered = dw[c] - average
        return total + centered * centered

    total = lax.fori_loop(0, chunks, squares, zero)
    variance = jnp.sum(total, axis=1, keepdims=True) * (1.0 / channels)
    inverse = lax.rsqrt(variance + 1e-05)

    def norm_step(c, carry):
        s1, s2 = carry
        lanes = at(c, LANES)
        normed = (dw[c] - average) * inverse
        affine = normed * gain_ref[:, lanes] + bias_ref[:, lanes]
        sig = jax.nn.sigmoid(affine)
        conv_out[:, lanes] = (affine * sig).astype(BF)
        affine_grad = og_v[:, lanes].astype(F32) * (sig * (1.0 + affine * (1.0 - sig)))
        part[c, taps : taps + 1, :] = jnp.sum(affine_grad * normed, axis=0, keepdims=True)
        part[c, taps + 1 : taps + 2, :] = jnp.sum(affine_grad, axis=0, keepdims=True)
        normed_grad = affine_grad * gain_ref[:, lanes]
        dw[c] = normed
        ng_s[c] = normed_grad
        return s1 + normed_grad, s2 + normed_grad * normed

    s1, s2 = lax.fori_loop(0, chunks, norm_step, (zero, zero))
    m1 = jnp.sum(s1, axis=1, keepdims=True) * (1.0 / channels)
    m2 = jnp.sum(s2, axis=1, keepdims=True) * (1.0 / channels)

    def depth_grad_step(c, carry):
        dg[c, 0:rows, :] = inverse * (ng_s[c] - m1 - dw[c] * m2)
        return carry

    lax.fori_loop(0, chunks, depth_grad_step, 0)
    halo2 = remote(
        dg.at[:, 0:HALO, :], dg.at[:, rows : rows + HALO, :], (dp, lax.rem(me + n_seq - 1, n_seq))
    )
    halo2.start()

    def glu_back(first, count):
        def body(c, carry):
            lanes = at(c, LANES)
            gates = pl.ds(pl.multiple_of(channels + c * LANES, LANES), LANES)
            here = slice(first, first + count)
            acc = jnp.zeros((count, LANES), F32)
            for o in range(taps):
                low = first + span - o
                acc = acc + taps_ref[o : o + 1, lanes] * dg[c, low : low + count, :]
            sig = sig_s[here, lanes]
            ig_out[here, lanes] = (acc * sig).astype(BF)
            slope = acc * a_s[here, lanes].astype(F32) * sig * (1.0 - sig)
            ig_out[here, gates] = slope.astype(BF)
            return carry

        lax.fori_loop(0, chunks, body, 0)

    glu_back(0, rows - HALO)
    halo2.wait_recv()
    halo2.wait_send()

    @pl.when(me == n_seq - 1)
    def _():
        dg[:, rows : rows + HALO, :] = jnp.zeros((chunks, HALO, LANES), F32)

    glu_back(rows - HALO, HALO)
    loads[1].wait()
    g_send = []
    for p in peers + [me]:
        cols = at(p, own)
        grad = lax.dot_general(
            ig_out[...], w_full[cols, :], (((1,), (1,)), ((), ())), preferred_element_type=F32
        )
        rg_out[:, cols] = (cg_v[:, cols].astype(F32) + grad).astype(BF)
        if p is me:
            g_h[at(me, rows), :] = rg_out[:, cols]
        else:
            copy = remote(rg_out.at[:, cols], g_h.at[at(me, rows), :], (dp, p))
            copy.start()
            g_send.append(copy)

    def tap_grad(c, carry):
        grad = dg[c, 0:rows, :]
        for o in range(taps):
            part[c, o : o + 1, :] = jnp.sum(
                grad * glu_f[c, base + o : base + o + rows, :], axis=0, keepdims=True
            )
        part[c, taps + 2 : TERM_ROWS, :] = jnp.zeros((TERM_ROWS - taps - 2, LANES), F32)
        return carry

    lax.fori_loop(0, chunks, tap_grad, 0)
    reduce1 = []
    for d, p in enumerate(dp_peers):
        copy = remote(part.at[p], rs_buf.at[d], (p, me))
        copy.start()
        reduce1.append(copy)

    for copy in g_send:
        copy.wait_recv()

    def backward_head(h):
        hr = slice(h * depth, (h + 1) * depth)
        slot = h % 2

        def body(b, carry):
            cols = at(b, q_block)
            grad = gt[hr, cols]
            dots = jnp.sum(
                grad.astype(F32) * ctxt[hr, cols].astype(F32), axis=0, keepdims=True
            )
            prob_grad = jnp.dot(v_h[:, hr], grad, preferred_element_type=F32)
            p = prob[h, :, cols]
            score_grad = (p * (prob_grad - dots) * scaling).astype(BF)
            ds_s[slot, :, cols] = score_grad
            dqt[hr, cols] = jnp.dot(kt[hr, :], score_grad, preferred_element_type=F32)
            return carry

        lax.fori_loop(0, frames // q_block, body, 0)

    first = lax.broadcasted_iota(jnp.int32, (frames, LANES), 1) < depth
    out_copies = []
    reduce2, reduce3 = [], []
    for pair in range(pairs):
        pc = slice(pair * LANES, (pair + 1) * LANES)
        left = jnp.dot(pb_s[2 * pair], g_h[:, pc], preferred_element_type=F32)
        right = jnp.dot(pb_s[2 * pair + 1], g_h[:, pc], preferred_element_type=F32)
        dv_h[:, pc] = jnp.where(first, left, right).astype(BF)
        out_copies.append(gather_pair(dv_h, dv_out, pair, 12 + pair))
        gt[pc, :] = flip(g_h[:, pc]).astype(BF)
    for pair in range(pairs):
        pc = slice(pair * LANES, (pair + 1) * LANES)
        backward_head(2 * pair)
        backward_head(2 * pair + 1)
        dq_h[:, pc] = dqt[pc, :].T.astype(BF)
        out_copies.append(gather_pair(dq_h, dq_out, pair, 14 + 2 * pair))
        left = jnp.dot(ds_s[0], q_h[:, pc], preferred_element_type=F32)
        right = jnp.dot(ds_s[1], q_h[:, pc], preferred_element_type=F32)
        dk_h[:, pc] = jnp.where(first, left, right).astype(BF)
        out_copies.append(gather_pair(dk_h, dk_out, pair, 15 + 2 * pair))
        if pair == 0:
            for copy in reduce1:
                copy.wait_recv()
            total = part[dp]
            for d in range(n_dp - 1):
                total = total + rs_buf[d]
            s2_buf[me] = total
            for p in peers:
                copy = remote(s2_buf.at[me], s2_buf.at[me], (dp, p))
                copy.start()
                reduce2.append(copy)

    for copy in reduce2:
        copy.wait_recv()
    total = s2_buf[0]
    for s in range(1, n_seq):
        total = total + s2_buf[s]
    fin[dp] = total * (1.0 / n_dp)
    for p in dp_peers:
        copy = remote(fin.at[dp], fin.at[dp], (p, me))
        copy.start()
        reduce3.append(copy)
    for copy in reduce3:
        copy.wait_recv()
    for c in range(chunks):
        lanes = slice(c * LANES, (c + 1) * LANES)
        kg_out[:, lanes] = fin[c, 0:taps, :]
        gg_out[:, lanes] = fin[c, taps : taps + 1, :]
        bg_out[:, lanes] = fin[c, taps + 1 : taps + 2, :]

    for copies, keep in out_copies:
        keep.wait()
        for copy in copies:
            copy.wait_recv()
    for copies, _ in sends + ctx_copies + out_copies:
        for copy in copies:
            copy.wait_send()
    for copy in (
        [w_mate] + w_across + w_x + w_fwd + g_send + reduce1 + reduce2 + reduce3
    ):
        copy.wait_send()


def place_outputs(*refs):
    sems = refs[20]
    copies = [pltpu.make_async_copy(refs[i], refs[10 + i], sems.at[i]) for i in range(10)]
    for copy in copies:
        copy.start()
    for copy in copies:
        copy.wait()


def fused_shards(
    queries, key_vecs, value_vecs, residual_in, point_weight, context_grad, depth_kernel,
    norm_gain, norm_bias, conv_grad,
):
    n_seq = lax.axis_size("seq")
    n_dp = lax.axis_size("dp")
    rows, channels = queries.shape[1:]
    taps = depth_kernel.shape[0]
    depth = channels // HEADS
    frames = rows * n_seq
    own = channels // n_seq
    heads = own // depth
    chunks = channels // LANES
    s = jax.ShapeDtypeStruct
    vm = pltpu.VMEM
    block = s((rows, channels), BF)
    head_rows = vm((frames, own), BF)
    head_cols = vm((own, frames), BF)
    n_copies = 112
    scratch = (
        [head_rows] * 4 + [head_cols] * 5 + [head_rows]
        + [vm((heads, frames, frames), F32), vm((heads, frames, frames), BF), vm((2, frames, frames), BF)]
        + [vm((own, frames), F32)] + [head_rows] * 3
        + [
            vm((rows, channels), BF),
            vm((rows, channels), BF),
            vm((rows, channels), BF),
            vm((channels, 2 * channels), BF),
            vm((rows, 2 * channels), F32),
            vm((rows, channels), BF),
            vm((rows, channels), BF),
            vm((rows, channels), F32),
            vm((chunks, HALO + rows, LANES), F32),
            vm((chunks, rows, LANES), F32),
            vm((chunks, rows, LANES), F32),
            vm((chunks, rows + HALO, LANES), F32),
            vm((chunks, TERM_ROWS, LANES), F32),
            vm((n_dp - 1, TERM_ROWS, LANES), F32),
            vm((n_seq, TERM_ROWS, LANES), F32),
            vm((chunks, TERM_ROWS, LANES), F32),
            pltpu.SemaphoreType.DMA((n_copies,)),
            pltpu.SemaphoreType.DMA((n_copies,)),
            pltpu.SemaphoreType.DMA((20,)),
        ]
    )
    spec = pl.BlockSpec(memory_space=pltpu.VMEM)
    hbm = pl.BlockSpec(memory_space=pl.ANY)
    outs = pl.pallas_call(
        functools.partial(fused_kernel, (n_seq, n_dp, rows, channels, taps, depth)),
        out_shape=(
            block, block, block, block, block, s((rows, 2 * channels), BF), block,
            s((taps, channels), F32), s((1, channels), F32), s((1, channels), F32),
        ),
        in_specs=[hbm] * 6 + [spec] * 3 + [hbm],
        out_specs=(spec,) * 10,
        scratch_shapes=scratch,
        compiler_params=pltpu.CompilerParams(
            collective_id=0, has_side_effects=True, vmem_limit_bytes=56 * 1024 * 1024
        ),
    )(
        queries[0], key_vecs[0], value_vecs[0], residual_in[0], point_weight, context_grad[0],
        depth_kernel, norm_gain[None], norm_bias[None], conv_grad[0],
    )
    outs = pl.pallas_call(
        place_outputs,
        out_shape=tuple(s(o.shape, o.dtype) for o in outs),
        in_specs=[hbm] * 10,
        out_specs=(hbm,) * 10,
        scratch_shapes=[pltpu.SemaphoreType.DMA((10,))],
    )(*outs)
    return tuple(o[None] for o in outs[:7]) + (outs[7], outs[8][0], outs[9][0])


def chosen(*args):
    n_seq = lax.axis_size("seq")
    n_dp = lax.axis_size("dp")
    recs, rows, channels = args[0].shape
    fits = (
        n_seq == 4
        and recs == 1
        and rows % 128 == 0
        and channels % (LANES * n_seq) == 0
        and 2 * channels == LANES * HEADS
        and channels // LANES == n_dp
        and rows * n_seq <= 512
        and args[4].shape[0] == channels // n_seq == 2 * LANES
        and args[6].shape[0] <= 31
    )
    return fused_shards(*args) if fits else shards(*args)


def solution(mesh):
    in_specs = (
        P("dp", "seq", None),
        P("dp", "seq", None),
        P("dp", "seq", None),
        P("dp", "seq", None),
        P("seq", None),
        P("dp", "seq", None),
        P(),
        P(),
        P(),
        P("dp", "seq", None),
    )
    out_specs = (
        P("dp", "seq", None),
        P("dp", "seq", None),
        P("dp", "seq", None),
        P("dp", "seq", None),
        P("dp", "seq", None),
        P("dp", "seq", None),
        P("dp", "seq", None),
        P(),
        P(),
        P(),
    )
    return jax.shard_map(chosen, mesh=mesh, in_specs=in_specs, out_specs=out_specs, check_vma=False)
```

```python
import functools
import jax
import jax.numpy as jnp
from jax import lax
from jax.sharding import PartitionSpec as P
from jax.experimental import pallas as pl
from jax.experimental.pallas import tpu as pltpu

HEADS = 16


def from_behind(block, axis, distance):
    devices = range(lax.axis_size(axis))
    route = [(i - distance, i) for i in devices if i - distance in devices]
    return lax.ppermute(block, axis, route)


def block_probs(query_block, key_heads, scaling):
    scores = (
        jnp.einsum("qhd,khd->hqk", query_block, key_heads, preferred_element_type=jnp.float32)
        * scaling
    )
    shifted = jnp.exp(scores - jnp.max(scores, axis=2, keepdims=True))
    return shifted / jnp.sum(shifted, axis=2, keepdims=True)


def attend_forward(query_part, key_part, value_part, head_count):
    frames, channels = query_part.shape
    head_depth = channels // head_count
    scaling = head_depth ** (-0.5)
    query_heads = query_part.reshape(frames, head_count, head_depth)
    key_heads = key_part.reshape(frames, head_count, head_depth)
    value_heads = value_part.reshape(frames, head_count, head_depth)
    block_rows = min(512, frames)

    def one_block(running, index):
        query_block = lax.dynamic_slice_in_dim(query_heads, index * block_rows, block_rows, 0)
        rounded = block_probs(query_block, key_heads, scaling).astype(jnp.bfloat16)
        context = jnp.einsum(
            "hqk,khd->qhd", rounded, value_heads, preferred_element_type=jnp.float32
        ).astype(jnp.bfloat16)
        return (running, context)

    unused, blocks = lax.scan(
        one_block, jnp.zeros((), jnp.float32), jnp.arange(frames // block_rows)
    )
    return blocks.reshape(frames, channels)


def attend_backward(query_part, key_part, value_part, grad_part, context_part, head_count):
    frames, channels = query_part.shape
    head_depth = channels // head_count
    scaling = head_depth ** (-0.5)
    query_heads = query_part.reshape(frames, head_count, head_depth)
    key_heads = key_part.reshape(frames, head_count, head_depth)
    value_heads = value_part.reshape(frames, head_count, head_depth)
    grad_heads = grad_part.reshape(frames, head_count, head_depth)
    context_heads = context_part.reshape(frames, head_count, head_depth)
    block_rows = min(512, frames)

    def one_block(running, index):
        key_total, value_total = running
        start = index * block_rows
        query_block = lax.dynamic_slice_in_dim(query_heads, start, block_rows, 0)
        grad_block = lax.dynamic_slice_in_dim(grad_heads, start, block_rows, 0)
        context_block = lax.dynamic_slice_in_dim(context_heads, start, block_rows, 0)
        probabilities = block_probs(query_block, key_heads, scaling)
        rounded = probabilities.astype(jnp.bfloat16)
        row_dots = jnp.sum(
            grad_block.astype(jnp.float32) * context_block.astype(jnp.float32), axis=2
        )
        prob_grad = jnp.einsum(
            "qhd,khd->hqk", grad_block, value_heads, preferred_element_type=jnp.float32
        )
        score_grad = (probabilities * (prob_grad - row_dots.T[:, :, None]) * scaling).astype(
            jnp.bfloat16
        )
        query_grad = jnp.einsum(
            "hqk,khd->qhd", score_grad, key_heads, preferred_element_type=jnp.float32
        ).astype(jnp.bfloat16)
        key_total = key_total + jnp.einsum(
            "hqk,qhd->khd", score_grad, query_block, preferred_element_type=jnp.float32
        )
        value_total = value_total + jnp.einsum(
            "hqk,qhd->khd", rounded, grad_block, preferred_element_type=jnp.float32
        )
        return ((key_total, value_total), query_grad)

    empty = jnp.zeros((frames, head_count, head_depth), jnp.float32)
    totals, blocks = lax.scan(one_block, (empty, empty), jnp.arange(frames // block_rows))
    query_grad = blocks.reshape(frames, channels)
    key_grad = totals[0].astype(jnp.bfloat16).reshape(frames, channels)
    value_grad = totals[1].astype(jnp.bfloat16).reshape(frames, channels)
    return (query_grad, key_grad, value_grad)


def shards(
    queries,
    key_vecs,
    value_vecs,
    residual_in,
    point_weight,
    context_grad,
    depth_kernel,
    norm_gain,
    norm_bias,
    conv_grad,
):
    head_count = HEADS // lax.axis_size("seq")
    query_heads, key_heads, value_heads = (
        lax.all_to_all(queries, "seq", split_axis=2, concat_axis=1, tiled=True),
        lax.all_to_all(key_vecs, "seq", split_axis=2, concat_axis=1, tiled=True),
        lax.all_to_all(value_vecs, "seq", split_axis=2, concat_axis=1, tiled=True),
    )
    context_local = attend_forward(query_heads[0], key_heads[0], value_heads[0], head_count)
    context_out = lax.all_to_all(
        context_local[None], "seq", split_axis=1, concat_axis=2, tiled=True
    )
    taps = depth_kernel.shape[0]
    channels = depth_kernel.shape[1]
    span = taps - 1
    frames = residual_in.shape[1]
    mixed = (residual_in[0].astype(jnp.float32) + context_out[0].astype(jnp.float32)).astype(
        jnp.bfloat16
    )
    pre_conv = jnp.dot(
        mixed,
        lax.all_gather(point_weight, "seq", axis=0, tiled=True),
        preferred_element_type=jnp.float32,
    )
    conv_input = pre_conv.astype(jnp.bfloat16)[None]
    value_half = conv_input[:, :, :channels].astype(jnp.float32)
    gate_sig = jax.nn.sigmoid(conv_input[:, :, channels:].astype(jnp.float32))
    glu = (value_half * gate_sig).astype(jnp.bfloat16)
    earlier = from_behind(glu[:, frames - span :], "seq", 1)
    glu_wide = jnp.concatenate([earlier, glu], axis=1)
    glu_view = lax.optimization_barrier(glu_wide).astype(jnp.float32)
    depthwise = jnp.zeros((1, frames, channels), jnp.float32)
    for offset in range(taps):
        depthwise = depthwise + depth_kernel[offset] * glu_view[:, offset : offset + frames]
    average = jnp.mean(depthwise, axis=2, keepdims=True)
    centered = depthwise - average
    variance = jnp.mean(centered * centered, axis=2, keepdims=True)
    inverse = lax.rsqrt(variance + 1e-05)
    normed = centered * inverse
    affine = normed * norm_gain + norm_bias
    sig_affine = jax.nn.sigmoid(affine)
    conv_output = (affine * sig_affine).astype(jnp.bfloat16)
    affine_grad = conv_grad.astype(jnp.float32) * (sig_affine * (1.0 + affine * (1.0 - sig_affine)))
    gain_term = jnp.sum(affine_grad * normed, axis=(0, 1))
    bias_term = jnp.sum(affine_grad, axis=(0, 1))
    normed_grad = affine_grad * norm_gain
    depth_grad = inverse * (
        normed_grad
        - jnp.mean(normed_grad, axis=2, keepdims=True)
        - normed * jnp.mean(normed_grad * normed, axis=2, keepdims=True)
    )
    kernel_term = jnp.stack(
        [
            jnp.sum(depth_grad * glu_view[:, offset : offset + frames], axis=(0, 1))
            for offset in range(taps)
        ]
    )
    kernel_total, gain_total, bias_total = lax.psum(
        (kernel_term, gain_term, bias_term), ("dp", "seq")
    )
    recordings = lax.axis_size("dp")
    kernel_grad = kernel_total / recordings
    gain_grad = gain_total / recordings
    bias_grad = bias_total / recordings
    later = from_behind(depth_grad[:, :span], "seq", -1)
    grad_wide = jnp.concatenate([depth_grad, later], axis=1)
    glu_grad = jnp.zeros((1, frames, channels), jnp.float32)
    for offset in range(taps):
        begin = span - offset
        glu_grad = glu_grad + depth_kernel[offset] * grad_wide[:, begin : begin + frames]
    input_grad = jnp.concatenate(
        [glu_grad * gate_sig, glu_grad * value_half * gate_sig * (1.0 - gate_sig)], axis=2
    ).astype(jnp.bfloat16)
    slope_rows = input_grad[0]
    mixed_grad = jnp.einsum(
        "fc,dc->fd",
        slope_rows,
        lax.all_gather(point_weight, "seq", axis=0, tiled=True),
        preferred_element_type=jnp.float32,
    )
    residual_grad = (context_grad.astype(jnp.float32) + mixed_grad[None]).astype(jnp.bfloat16)
    grad_heads = lax.all_to_all(residual_grad, "seq", split_axis=2, concat_axis=1, tiled=True)
    query_grad, key_grad, value_grad = attend_backward(
        query_heads[0], key_heads[0], value_heads[0], grad_heads[0], context_local, head_count
    )
    query_out, key_out, value_out = (
        lax.all_to_all(query_grad[None], "seq", split_axis=1, concat_axis=2, tiled=True),
        lax.all_to_all(key_grad[None], "seq", split_axis=1, concat_axis=2, tiled=True),
        lax.all_to_all(value_grad[None], "seq", split_axis=1, concat_axis=2, tiled=True),
    )
    return (
        context_out,
        conv_output,
        query_out,
        key_out,
        value_out,
        input_grad,
        residual_grad,
        kernel_grad,
        gain_grad,
        bias_grad,
    )


BF = jnp.bfloat16
F32 = jnp.float32
HALO = 32
LANES = 128
TERM_ROWS = 40


def fused_kernel(
    dims,
    q_ref, k_ref, v_ref, res_ref, w_ref, cg_ref, taps_ref, gain_ref, bias_ref, og_ref,
    ctx_out, conv_out, dq_out, dk_out, dv_out, ig_out, rg_out, kg_out, gg_out, bg_out,
    q_h, k_h, v_h, g_h, qt, kt, vt, gt, ctxt, ctx_h, prob, pb_s, ds_s, dqt, dq_h, dk_h, dv_h,
    res_v, cg_v, og_v, w_full, pre, mixed, a_s, sig_s, glu_f, dw, ng_s, dg, part, rs_buf, s2_buf, fin,
    ssem, rsem, lsem,
):
    n_seq, n_dp, rows, channels, taps, depth = dims
    own = channels // n_seq
    pairs = own // LANES
    frames = rows * n_seq
    chunks = channels // LANES
    scaling = depth ** (-0.5)
    me = lax.axis_index("seq")
    dp = lax.axis_index("dp")
    core = lax.rem(me, 2)
    mate = me + 1 - 2 * core
    across = lax.rem(me + 2, n_seq)
    x_pos = lax.rem(dp, 2)
    x_dp = dp + 1 - 2 * x_pos
    counter = [0]

    def remote(src, dst, device):
        index = counter[0]
        counter[0] += 1
        return pltpu.make_async_remote_copy(
            src_ref=src, dst_ref=dst, send_sem=ssem.at[index], recv_sem=rsem.at[index],
            device_id=device, device_id_type=pl.DeviceIdType.MESH,
        )

    diag = lax.rem(mate + 2, n_seq)
    chip = lax.div(me, 2)
    peers = [across, diag, mate]
    dp_peers = [lax.rem(dp + d, n_dp) for d in range(1, n_dp)]
    barrier = pltpu.get_barrier_semaphore()
    for p in peers:
        pl.semaphore_signal(barrier, inc=1, device_id=(dp, p), device_id_type=pl.DeviceIdType.MESH)
    for p in dp_peers:
        pl.semaphore_signal(barrier, inc=1, device_id=(p, me), device_id_type=pl.DeviceIdType.MESH)
    pl.semaphore_wait(barrier, n_seq - 1 + n_dp - 1)

    def at(value, size):
        return pl.ds(pl.multiple_of(value * size, size), size)

    loads = []
    for t, (src, dst) in enumerate(((res_ref, res_v), (cg_ref, cg_v), (og_ref, og_v))):
        copy = pltpu.make_async_copy(src, dst, lsem.at[t])
        copy.start()
        loads.append(copy)

    def head_cols(owner, pair):
        return pl.ds(pl.multiple_of(owner * own + pair * LANES, LANES), LANES)

    sends = []
    for pair in range(pairs):
        pc = slice(pair * LANES, (pair + 1) * LANES)
        for t, (src, dst) in enumerate(((q_ref, q_h), (k_ref, k_h), (v_ref, v_h))):
            copies = []
            for p in peers:
                copy = remote(src.at[:, head_cols(p, pair)], dst.at[at(me, rows), pc], (dp, p))
                copy.start()
                copies.append(copy)
            keep = pltpu.make_async_copy(
                src.at[:, head_cols(me, pair)], dst.at[at(me, rows), pc], lsem.at[4 + 3 * pair + t]
            )
            keep.start()
            sends.append((copies, keep))

    w_rows = w_ref.shape[0]
    half = w_rows // 2
    pieces = 4
    piece = half // pieces
    w_mate = remote(w_ref, w_full.at[at(me, w_rows), :], (dp, mate))
    w_mate.start()
    w_self = pltpu.make_async_copy(w_ref, w_full.at[at(me, w_rows), :], lsem.at[3])
    w_self.start()
    w_across = []
    for j in range(pieces):
        start = pl.multiple_of(x_pos * half + j * piece, piece)
        copy = remote(
            w_ref.at[pl.ds(start, piece), :],
            w_full.at[pl.ds(pl.multiple_of(me * w_rows + start, piece), piece), :],
            (dp, across),
        )
        copy.start()
        w_across.append(copy)

    def flip(value):
        return value.astype(F32).T

    def arrive(index):
        copies, keep = sends[index]
        keep.wait()
        for copy in copies:
            copy.wait_recv()

    q_block = min(256, frames)

    def forward_head(h):
        hr = slice(h * depth, (h + 1) * depth)

        def body(b, carry):
            cols = at(b, q_block)
            scores = jnp.dot(k_h[:, hr], qt[hr, cols], preferred_element_type=F32)
            shifted = jnp.exp(scores - jnp.max(scores, axis=0, keepdims=True))
            p = shifted * (1.0 / jnp.sum(shifted, axis=0, keepdims=True))
            rounded = p.astype(BF)
            prob[h, :, cols] = p
            pb_s[h, :, cols] = rounded
            ctxt[hr, cols] = jnp.dot(vt[hr, :], rounded, preferred_element_type=F32).astype(BF)
            return carry

        lax.fori_loop(0, frames // q_block, body, 0)

    def gather_pair(src, dst, pair, t):
        copies = []
        source = slice(pair * LANES, (pair + 1) * LANES)
        for p in peers:
            copy = remote(src.at[at(p, rows), source], dst.at[:, head_cols(me, pair)], (dp, p))
            copy.start()
            copies.append(copy)
        keep = pltpu.make_async_copy(
            src.at[at(me, rows), source], dst.at[:, head_cols(me, pair)], lsem.at[t]
        )
        keep.start()
        return copies, keep

    ctx_copies = []
    for pair in range(pairs):
        pc = slice(pair * LANES, (pair + 1) * LANES)
        arrive(3 * pair)
        qt[pc, :] = (flip(q_h[:, pc]) * scaling).astype(BF)
        arrive(3 * pair + 1)
        arrive(3 * pair + 2)
        vt[pc, :] = flip(v_h[:, pc]).astype(BF)
        forward_head(2 * pair)
        forward_head(2 * pair + 1)
        ctx_h[:, pc] = flip(ctxt[pc, :]).astype(BF)
        ctx_copies.append(gather_pair(ctx_h, ctx_out, pair, 10 + pair))

    def w_part(owner, side, j):
        return pl.ds(pl.multiple_of(owner * w_rows + side * half + j * piece, piece), piece)

    def forward(here, device):
        copy = remote(w_full.at[here, :], w_full.at[here, :], device)
        copy.start()
        return copy

    w_x, w_fwd = [], []
    for j in range(pieces):
        w_across[j].wait_recv()
        here = w_part(across, x_pos, j)
        w_x.append(forward(here, (x_dp, me)))
        w_fwd.append(forward(here, (dp, mate)))
        if j == 0:
            for pair in range(pairs):
                pc = slice(pair * LANES, (pair + 1) * LANES)
                kt[pc, :] = flip(k_h[:, pc]).astype(BF)

    for copies, keep in ctx_copies:
        keep.wait()
        copies[2].wait_recv()
    loads[0].wait()
    w_self.wait()
    w_mate.wait_recv()
    near = at(chip, 2 * own)
    far = at(1 - chip, 2 * own)
    wide = 2 * LANES
    mixed[:, near] = (res_v[:, near].astype(F32) + ctx_out[:, near].astype(F32)).astype(BF)

    def conv_near(i, carry):
        cols = at(i, wide)
        pre[:, cols] = jnp.dot(mixed[:, near], w_full[near, cols], preferred_element_type=F32)
        return carry

    lax.fori_loop(0, 2 * channels // wide, conv_near, 0)
    for j in range(pieces):
        w_x[j].wait_recv()
        w_fwd.append(forward(w_part(across, 1 - x_pos, j), (dp, mate)))
    for copies, keep in ctx_copies:
        copies[0].wait_recv()
        copies[1].wait_recv()
    mixed[:, far] = (res_v[:, far].astype(F32) + ctx_out[:, far].astype(F32)).astype(BF)
    for copy in w_fwd:
        copy.wait_recv()

    def conv_in(i, carry):
        cols = at(i, wide)
        gates = pl.ds(pl.multiple_of(channels + i * wide, wide), wide)
        a = jnp.dot(mixed[:, far], w_full[far, cols], preferred_element_type=F32)
        b = jnp.dot(mixed[:, far], w_full[far, gates], preferred_element_type=F32)
        a = (a + pre[:, cols]).astype(BF)
        b = (b + pre[:, gates]).astype(BF)
        sig = jax.nn.sigmoid(b.astype(F32))
        a_s[:, cols] = a
        sig_s[:, cols] = sig
        glu = (a.astype(F32) * sig).astype(BF).astype(F32)
        glu_f[2 * i, HALO : HALO + rows, :] = glu[:, :LANES]
        glu_f[2 * i + 1, HALO : HALO + rows, :] = glu[:, LANES:]
        return carry

    lax.fori_loop(0, channels // wide, conv_in, 0)
    halo1 = remote(
        glu_f.at[:, rows : rows + HALO, :], glu_f.at[:, 0:HALO, :], (dp, lax.rem(me + 1, n_seq))
    )
    halo1.start()
    span = taps - 1
    base = HALO - span

    def depth_rows(first, count):
        def body(c, total):
            lanes = at(c, LANES)
            acc = jnp.zeros((count, LANES), F32)
            for o in range(taps):
                low = base + first + o
                acc = acc + taps_ref[o : o + 1, lanes] * glu_f[c, low : low + count, :]
            dw[c, first : first + count, :] = acc
            return total + acc

        return lax.fori_loop(0, chunks, body, jnp.zeros((count, LANES), F32))

    total_late = depth_rows(HALO, rows - HALO)
    halo1.wait_recv()
    halo1.wait_send()

    @pl.when(me == 0)
    def _():
        glu_f[:, 0:HALO, :] = jnp.zeros((chunks, HALO, LANES), F32)

    total_early = depth_rows(0, HALO)
    average = jnp.concatenate(
        [jnp.sum(total_early, axis=1, keepdims=True), jnp.sum(total_late, axis=1, keepdims=True)],
        axis=0,
    ) * (1.0 / channels)
    zero = jnp.zeros((rows, LANES), F32)
    loads[2].wait()

    def squares(c, total):
        centered = dw[c] - average
        return total + centered * centered

    total = lax.fori_loop(0, chunks, squares, zero)
    variance = jnp.sum(total, axis=1, keepdims=True) * (1.0 / channels)
    inverse = lax.rsqrt(variance + 1e-05)

    def norm_step(c, carry):
        s1, s2 = carry
        lanes = at(c, LANES)
        normed = (dw[c] - average) * inverse
        affine = normed * gain_ref[:, lanes] + bias_ref[:, lanes]
        sig = jax.nn.sigmoid(affine)
        conv_out[:, lanes] = (affine * sig).astype(BF)
        affine_grad = og_v[:, lanes].astype(F32) * (sig * (1.0 + affine * (1.0 - sig)))
        part[c, taps : taps + 1, :] = jnp.sum(affine_grad * normed, axis=0, keepdims=True)
        part[c, taps + 1 : taps + 2, :] = jnp.sum(affine_grad, axis=0, keepdims=True)
        normed_grad = affine_grad * gain_ref[:, lanes]
        dw[c] = normed
        ng_s[c] = normed_grad
        return s1 + normed_grad, s2 + normed_grad * normed

    s1, s2 = lax.fori_loop(0, chunks, norm_step, (zero, zero))
    m1 = jnp.sum(s1, axis=1, keepdims=True) * (1.0 / channels)
    m2 = jnp.sum(s2, axis=1, keepdims=True) * (1.0 / channels)

    def depth_grad_step(c, carry):
        dg[c, 0:rows, :] = inverse * (ng_s[c] - m1 - dw[c] * m2)
        return carry

    lax.fori_loop(0, chunks, depth_grad_step, 0)
    halo2 = remote(
        dg.at[:, 0:HALO, :], dg.at[:, rows : rows + HALO, :], (dp, lax.rem(me + n_seq - 1, n_seq))
    )
    halo2.start()

    def glu_back(first, count):
        def body(c, carry):
            lanes = at(c, LANES)
            gates = pl.ds(pl.multiple_of(channels + c * LANES, LANES), LANES)
            here = slice(first, first + count)
            acc = jnp.zeros((count, LANES), F32)
            for o in range(taps):
                low = first + span - o
                acc = acc + taps_ref[o : o + 1, lanes] * dg[c, low : low + count, :]
            sig = sig_s[here, lanes]
            ig_out[here, lanes] = (acc * sig).astype(BF)
            slope = acc * a_s[here, lanes].astype(F32) * sig * (1.0 - sig)
            ig_out[here, gates] = slope.astype(BF)
            return carry

        lax.fori_loop(0, chunks, body, 0)

    glu_back(0, rows - HALO)
    halo2.wait_recv()
    halo2.wait_send()

    @pl.when(me == n_seq - 1)
    def _():
        dg[:, rows : rows + HALO, :] = jnp.zeros((chunks, HALO, LANES), F32)

    glu_back(rows - HALO, HALO)
    loads[1].wait()
    g_send = []
    for p in peers + [me]:
        cols = at(p, own)
        grad = lax.dot_general(
            ig_out[...], w_full[cols, :], (((1,), (1,)), ((), ())), preferred_element_type=F32
        )
        rg_out[:, cols] = (cg_v[:, cols].astype(F32) + grad).astype(BF)
        if p is me:
            g_h[at(me, rows), :] = rg_out[:, cols]
        else:
            copy = remote(rg_out.at[:, cols], g_h.at[at(me, rows), :], (dp, p))
            copy.start()
            g_send.append(copy)

    def tap_grad(c, carry):
        grad = dg[c, 0:rows, :]
        for o in range(taps):
            part[c, o : o + 1, :] = jnp.sum(
                grad * glu_f[c, base + o : base + o + rows, :], axis=0, keepdims=True
            )
        part[c, taps + 2 : TERM_ROWS, :] = jnp.zeros((TERM_ROWS - taps - 2, LANES), F32)
        return carry

    lax.fori_loop(0, chunks, tap_grad, 0)
    reduce1 = []
    for d, p in enumerate(dp_peers):
        copy = remote(part.at[p], rs_buf.at[d], (p, me))
        copy.start()
        reduce1.append(copy)

    for copy in g_send:
        copy.wait_recv()

    def backward_head(h):
        hr = slice(h * depth, (h + 1) * depth)
        slot = h % 2

        def body(b, carry):
            cols = at(b, q_block)
            grad = gt[hr, cols]
            dots = jnp.sum(
                grad.astype(F32) * ctxt[hr, cols].astype(F32), axis=0, keepdims=True
            )
            prob_grad = jnp.dot(v_h[:, hr], grad, preferred_element_type=F32)
            p = prob[h, :, cols]
            score_grad = (p * (prob_grad - dots) * scaling).astype(BF)
            ds_s[slot, :, cols] = score_grad
            dqt[hr, cols] = jnp.dot(kt[hr, :], score_grad, preferred_element_type=F32)
            return carry

        lax.fori_loop(0, frames // q_block, body, 0)

    first = lax.broadcasted_iota(jnp.int32, (frames, LANES), 1) < depth
    out_copies = []
    reduce2, reduce3 = [], []
    for pair in range(pairs):
        pc = slice(pair * LANES, (pair + 1) * LANES)
        left = jnp.dot(pb_s[2 * pair], g_h[:, pc], preferred_element_type=F32)
        right = jnp.dot(pb_s[2 * pair + 1], g_h[:, pc], preferred_element_type=F32)
        dv_h[:, pc] = jnp.where(first, left, right).astype(BF)
        out_copies.append(gather_pair(dv_h, dv_out, pair, 12 + pair))
        gt[pc, :] = flip(g_h[:, pc]).astype(BF)
    for copy in reduce1:
        copy.wait_recv()
    total = part[dp]
    for d in range(n_dp - 1):
        total = total + rs_buf[d]
    s2_buf[me] = total
    for p in peers:
        copy = remote(s2_buf.at[me], s2_buf.at[me], (dp, p))
        copy.start()
        reduce2.append(copy)
    for pair in range(pairs):
        pc = slice(pair * LANES, (pair + 1) * LANES)
        backward_head(2 * pair)
        backward_head(2 * pair + 1)
        dq_h[:, pc] = dqt[pc, :].T.astype(BF)
        out_copies.append(gather_pair(dq_h, dq_out, pair, 14 + 2 * pair))
        left = jnp.dot(ds_s[0], q_h[:, pc], preferred_element_type=F32)
        right = jnp.dot(ds_s[1], q_h[:, pc], preferred_element_type=F32)
        dk_h[:, pc] = jnp.where(first, left, right).astype(BF)
        out_copies.append(gather_pair(dk_h, dk_out, pair, 15 + 2 * pair))
        if pair == 0:
            for copy in reduce2:
                copy.wait_recv()
            total = s2_buf[0]
            for s in range(1, n_seq):
                total = total + s2_buf[s]
            fin[dp] = total * (1.0 / n_dp)
            for p in dp_peers:
                copy = remote(fin.at[dp], fin.at[dp], (p, me))
                copy.start()
                reduce3.append(copy)

    for copy in reduce3:
        copy.wait_recv()
    for c in range(chunks):
        lanes = slice(c * LANES, (c + 1) * LANES)
        kg_out[:, lanes] = fin[c, 0:taps, :]
        gg_out[:, lanes] = fin[c, taps : taps + 1, :]
        bg_out[:, lanes] = fin[c, taps + 1 : taps + 2, :]

    for copies, keep in out_copies:
        keep.wait()
        for copy in copies:
            copy.wait_recv()
    for copies, _ in sends + ctx_copies + out_copies:
        for copy in copies:
            copy.wait_send()
    for copy in (
        [w_mate] + w_across + w_x + w_fwd + g_send + reduce1 + reduce2 + reduce3
    ):
        copy.wait_send()


def place_outputs(*refs):
    sems = refs[20]
    copies = [pltpu.make_async_copy(refs[i], refs[10 + i], sems.at[i]) for i in range(10)]
    for copy in copies:
        copy.start()
    for copy in copies:
        copy.wait()


def fused_shards(
    queries, key_vecs, value_vecs, residual_in, point_weight, context_grad, depth_kernel,
    norm_gain, norm_bias, conv_grad,
):
    n_seq = lax.axis_size("seq")
    n_dp = lax.axis_size("dp")
    rows, channels = queries.shape[1:]
    taps = depth_kernel.shape[0]
    depth = channels // HEADS
    frames = rows * n_seq
    own = channels // n_seq
    heads = own // depth
    chunks = channels // LANES
    s = jax.ShapeDtypeStruct
    vm = pltpu.VMEM
    block = s((rows, channels), BF)
    head_rows = vm((frames, own), BF)
    head_cols = vm((own, frames), BF)
    n_copies = 112
    scratch = (
        [head_rows] * 4 + [head_cols] * 5 + [head_rows]
        + [vm((heads, frames, frames), F32), vm((heads, frames, frames), BF), vm((2, frames, frames), BF)]
        + [vm((own, frames), F32)] + [head_rows] * 3
        + [
            vm((rows, channels), BF),
            vm((rows, channels), BF),
            vm((rows, channels), BF),
            vm((channels, 2 * channels), BF),
            vm((rows, 2 * channels), F32),
            vm((rows, channels), BF),
            vm((rows, channels), BF),
            vm((rows, channels), F32),
            vm((chunks, HALO + rows, LANES), F32),
            vm((chunks, rows, LANES), F32),
            vm((chunks, rows, LANES), F32),
            vm((chunks, rows + HALO, LANES), F32),
            vm((chunks, TERM_ROWS, LANES), F32),
            vm((n_dp - 1, TERM_ROWS, LANES), F32),
            vm((n_seq, TERM_ROWS, LANES), F32),
            vm((chunks, TERM_ROWS, LANES), F32),
            pltpu.SemaphoreType.DMA((n_copies,)),
            pltpu.SemaphoreType.DMA((n_copies,)),
            pltpu.SemaphoreType.DMA((20,)),
        ]
    )
    spec = pl.BlockSpec(memory_space=pltpu.VMEM)
    hbm = pl.BlockSpec(memory_space=pl.ANY)
    outs = pl.pallas_call(
        functools.partial(fused_kernel, (n_seq, n_dp, rows, channels, taps, depth)),
        out_shape=(
            block, block, block, block, block, s((rows, 2 * channels), BF), block,
            s((taps, channels), F32), s((1, channels), F32), s((1, channels), F32),
        ),
        in_specs=[hbm] * 6 + [spec] * 3 + [hbm],
        out_specs=(spec,) * 10,
        scratch_shapes=scratch,
        compiler_params=pltpu.CompilerParams(
            collective_id=0, has_side_effects=True, vmem_limit_bytes=56 * 1024 * 1024
        ),
    )(
        queries[0], key_vecs[0], value_vecs[0], residual_in[0], point_weight, context_grad[0],
        depth_kernel, norm_gain[None], norm_bias[None], conv_grad[0],
    )
    outs = pl.pallas_call(
        place_outputs,
        out_shape=tuple(s(o.shape, o.dtype) for o in outs),
        in_specs=[spec] * 10,
        out_specs=(hbm,) * 10,
        scratch_shapes=[pltpu.SemaphoreType.DMA((10,))],
    )(*outs)
    return tuple(o[None] for o in outs[:7]) + (outs[7], outs[8][0], outs[9][0])


def chosen(*args):
    n_seq = lax.axis_size("seq")
    n_dp = lax.axis_size("dp")
    recs, rows, channels = args[0].shape
    fits = (
        n_seq == 4
        and recs == 1
        and rows % 128 == 0
        and channels % (LANES * n_seq) == 0
        and 2 * channels == LANES * HEADS
        and channels // LANES == n_dp
        and rows * n_seq <= 512
        and args[4].shape[0] == channels // n_seq == 2 * LANES
        and args[6].shape[0] <= 31
    )
    return fused_shards(*args) if fits else shards(*args)


def solution(mesh):
    in_specs = (
        P("dp", "seq", None),
        P("dp", "seq", None),
        P("dp", "seq", None),
        P("dp", "seq", None),
        P("seq", None),
        P("dp", "seq", None),
        P(),
        P(),
        P(),
        P("dp", "seq", None),
    )
    out_specs = (
        P("dp", "seq", None),
        P("dp", "seq", None),
        P("dp", "seq", None),
        P("dp", "seq", None),
        P("dp", "seq", None),
        P("dp", "seq", None),
        P("dp", "seq", None),
        P(),
        P(),
        P(),
    )
    return jax.shard_map(chosen, mesh=mesh, in_specs=in_specs, out_specs=out_specs, check_vma=False)
```
